256 devices in a mesh: dp: 4 (over y), segment: 8 (over z_hi, x), chan: 8 (over z_lo, core).
Axes of the slice: x: 4, y: 4, z: 8 (z_hi: 2, z_lo: 4; z = z_hi * 4 + z_lo), core: 2. Of those that a mesh axis runs over, the one named last changes fastest.
Arguments:
- x_input: bfloat16 [4, 4, 256, 1024], P(None, 'dp', None, 'chan'), may hold values from -48 to 48
- d_output: bfloat16 [4, 4, 256, 1024], P(None, 'dp', None, 'chan'), may hold values from -6 to 6
- weights: bfloat16 [8, 9, 1024, 1024], P('segment', None, None, 'chan'), may hold values from -0.0625 to 0.0625
- gains: float32 [8, 1024], P('segment', 'chan'), may hold values from 0.5 to 1.5
- biases: float32 [8, 1024], P('segment', 'chan'), may hold values from -3 to 3
Outputs:
- d_weights: float32 [8, 9, 1024, 1024], P('segment', None, None, 'chan')
- d_gains: float32 [8, 1024], P('segment', 'chan')
- d_biases: float32 [8, 1024], P('segment', 'chan')
The draws below stay inside these ranges and needn't reach their ends.
All inputs are finite; a program needn't handle non-finite values.
Results may differ from the reference program's by a relative error of at most 0.025.
Values may be sent and summed in bfloat16 or wider, within the bound.
No kernel may reach another device: no remote copies, remote signals or barrier semaphores. Data moves between devices by JAX's collectives and lax.ppermute only.
A program may use at most 64 MiB of HBM per device.

```python
import jax
import jax.numpy as jnp
from jax import lax

C = 1024
GROUPS = 32
SIDE = 16
MICRO = 4
IMAGES = 4
SECTIONS = 8
N_CHAN = 8


def draw_x_input(key, part):
    key_base, key_chan, key_pixel = jax.random.split(key, 3)
    base_values = jax.random.truncated_normal(key_base, -4.0, 4.0, (MICRO, IMAGES, SIDE * SIDE, C), jnp.float32)
    chan_scale = jnp.exp(jax.random.uniform(key_chan, (C,), jnp.float32, jnp.log(0.5), jnp.log(5.0)))
    pixel_scale = jnp.exp(jax.random.uniform(key_pixel, (MICRO, IMAGES, SIDE * SIDE, 1), jnp.float32, jnp.log(0.5), jnp.log(2.0)))
    values = base_values * chan_scale * pixel_scale
    return values.astype(jnp.bfloat16)


def levels(key, dims, cuts, smallest, largest):
    factor_of, own = 1.0, jax.random.fold_in(key, 6)
    for dim, shards_of in cuts:
        heights = jnp.exp(jax.random.uniform(jax.random.fold_in(own, dim), (shards_of,), jnp.float32, smallest / len(cuts), largest / len(cuts)))
        factor_of = factor_of * jnp.repeat(heights, dims[dim] // shards_of).reshape([-1 if axis == dim else 1 for axis in range(len(dims))])
    return factor_of


def scatter_about(stream_key, shape, width, bound, cuts=(), held_as=jnp.bfloat16):
    entries = width * jax.random.normal(stream_key, shape, jnp.float32)
    if cuts:
        entries = entries * levels(stream_key, shape, cuts, -0.22, 0.18)
    return jnp.clip(entries, -bound, bound).astype(held_as)


def setup_inputs(seed: int = 0) -> dict:
    arg_keys = jax.random.split(jax.random.key(seed), 6)
    return {
        "x_input": draw_x_input(jax.random.fold_in(arg_keys[5], 71), 0),
        "d_output": scatter_about(arg_keys[1], (MICRO, IMAGES, SIDE * SIDE, C), 1.0, 6.0, ((1, 4), (3, 8))),
        "weights": scatter_about(arg_keys[2], (SECTIONS, 9, C, C), (9 * C) ** -0.5, 0.0625, ((0, 8), (3, 8))),
        "gains": jnp.clip(1.0 + 0.1 * jax.random.normal(arg_keys[3], (SECTIONS, C), jnp.float32), 0.5, 1.5),
        "biases": scatter_about(arg_keys[4], (SECTIONS, C), 0.5, 3.0, ((0, 8), (1, 8)), jnp.float32),
    }


EPSILON = 1e-05

def expand_groups(statistic, channels):
    return jnp.repeat(statistic, channels // GROUPS, axis=1)[:, None, :]

def group_means(values):
    batch_count, pixel_count, channels = values.shape
    grouped = values.reshape(batch_count, pixel_count, GROUPS, channels // GROUPS)
    return lax.optimization_barrier(jnp.mean(grouped, axis=(1, 3)))

def shifted_stack(images, forward_taps):
    batch_count, pixel_count, channels = images.shape
    square = images.reshape(batch_count, SIDE, SIDE, channels)
    padded = jnp.pad(square, ((0, 0), (1, 1), (1, 1), (0, 0)))
    tap_list = []
    for tap_y in range(3):
        for tap_x in range(3):
            start_y = tap_y if forward_taps else 2 - tap_y
            start_x = tap_x if forward_taps else 2 - tap_x
            window = padded[:, start_y:start_y + SIDE, start_x:start_x + SIDE, :]
            tap_list.append(window.reshape(batch_count * pixel_count, channels))
    return jnp.stack(tap_list)

def block_forward(inputs, weight, gain_row, bias_row):
    values = inputs.astype(jnp.float32)
    group_mean = group_means(values)
    centred = values - expand_groups(group_mean, C)
    group_rstd = lax.rsqrt(group_means(centred * centred) + EPSILON)
    normed = centred * expand_groups(group_rstd, C)
    pre_act = normed * gain_row + bias_row
    hidden = (pre_act * jax.nn.sigmoid(pre_act)).astype(jnp.bfloat16)
    tap_stack = shifted_stack(hidden, True).astype(jnp.float32)
    conv_out = jnp.einsum('trc,tco->ro', tap_stack, weight.astype(jnp.float32), precision=lax.Precision.HIGHEST)
    output = (values + conv_out.reshape(values.shape)).astype(jnp.bfloat16)
    return (output, (inputs, group_mean, group_rstd))

def block_backward(grad_out, saved, weight, gain_row, bias_row):
    inputs, group_mean, group_rstd = saved
    values = inputs.astype(jnp.float32)
    normed = (values - expand_groups(group_mean, C)) * expand_groups(group_rstd, C)
    pre_act = normed * gain_row + bias_row
    sigma = jax.nn.sigmoid(pre_act)
    hidden = (pre_act * sigma).astype(jnp.bfloat16)
    grad_rows = grad_out.reshape(-1, C).astype(jnp.float32)
    grad_weight = jnp.einsum('trc,ro->tco', shifted_stack(hidden, True).astype(jnp.float32), grad_rows, precision=lax.Precision.HIGHEST)
    back_stack = shifted_stack(grad_out, False).astype(jnp.float32)
    row_total = back_stack.shape[1]
    block_width = C // N_CHAN
    back_blocks = back_stack.reshape(9, row_total, N_CHAN, block_width)
    weight_blocks = weight.astype(jnp.float32).reshape(9, C, N_CHAN, block_width)
    partials = jnp.einsum('trkp,tckp->krc', back_blocks, weight_blocks, precision=lax.Precision.HIGHEST)
    partials = partials.astype(jnp.bfloat16).astype(jnp.float32)
    grad_hidden = lax.optimization_barrier(jnp.sum(partials, axis=0)).reshape(values.shape)
    grad_pre = grad_hidden * sigma * (1.0 + pre_act * (1.0 - sigma))
    grad_gain = lax.optimization_barrier(jnp.sum(grad_pre * normed, axis=(0, 1)))
    grad_bias = lax.optimization_barrier(jnp.sum(grad_pre, axis=(0, 1)))
    grad_normed = grad_pre * gain_row
    first_mean = group_means(grad_normed)
    second_mean = group_means(grad_normed * normed)
    grad_in = grad_out.astype(jnp.float32) + expand_groups(group_rstd, C) * (grad_normed - expand_groups(first_mean, C) - normed * expand_groups(second_mean, C))
    return (grad_in.astype(jnp.bfloat16), grad_weight, grad_gain, grad_bias)

def reference(x_input, d_output, weights, gains, biases):
    sections = weights.shape[0]
    half_way = sections // 2
    weight_sums = [jnp.zeros((9, C, C), jnp.float32) for section in range(sections)]
    gain_sums = [jnp.zeros((C,), jnp.float32) for section in range(sections)]
    bias_sums = [jnp.zeros((C,), jnp.float32) for section in range(sections)]
    for micro_index in range(MICRO):
        saved_list = [None] * sections
        skip_list = []
        current = x_input[micro_index]
        for section in range(half_way):
            current, saved_list[section] = block_forward(current, weights[section], gains[section], biases[section])
            skip_list.append(current)
        upward = jnp.zeros_like(current)
        for branch in reversed(range(half_way)):
            joined = (upward.astype(jnp.float32) + skip_list[branch].astype(jnp.float32)).astype(jnp.bfloat16)
            section = 2 * half_way - 1 - branch
            upward, saved_list[section] = block_forward(joined, weights[section], gains[section], biases[section])
        grad_now = d_output[micro_index]
        skip_grads = []
        for branch in range(half_way):
            section = 2 * half_way - 1 - branch
            grad_now, grad_weight, grad_gain, grad_bias = block_backward(grad_now, saved_list[section], weights[section], gains[section], biases[section])
            weight_sums[section] = weight_sums[section] + grad_weight
            gain_sums[section] = gain_sums[section] + grad_gain
            bias_sums[section] = bias_sums[section] + grad_bias
            skip_grads.append(grad_now)
        later_grad = None
        for section in reversed(range(half_way)):
            if section == half_way - 1:
                grad_now = skip_grads[section]
            else:
                grad_now = (skip_grads[section].astype(jnp.float32) + later_grad.astype(jnp.float32)).astype(jnp.bfloat16)
            later_grad, grad_weight, grad_gain, grad_bias = block_backward(grad_now, saved_list[section], weights[section], gains[section], biases[section])
            weight_sums[section] = weight_sums[section] + grad_weight
            gain_sums[section] = gain_sums[section] + grad_gain
            bias_sums[section] = bias_sums[section] + grad_bias
    return (jnp.stack(weight_sums), jnp.stack(gain_sums), jnp.stack(bias_sums))
```

```python
import jax
import jax.numpy as jnp
from jax import lax
from jax.experimental import pallas as pl
from jax.experimental.pallas import tpu as pltpu
from jax.sharding import PartitionSpec as P

GROUPS = 32
SIDE = 16
EPSILON = 1e-05
PIX = SIDE * SIDE
BF = jnp.bfloat16
F32 = jnp.float32


def _groups(width):
    r = lax.broadcasted_iota(jnp.int32, (128, 128), 0) // width
    c = lax.broadcasted_iota(jnp.int32, (128, 128), 1) // width
    return jnp.where(r == c, 1.0, 0.0).astype(BF)


def _group_sum(v, ones):
    n = v.shape[1] // 128
    rows = jnp.concatenate([v[:, i * 128:(i + 1) * 128] for i in range(n)], axis=0)
    hi = rows.astype(BF)
    rest = rows - hi.astype(F32)
    mid = rest.astype(BF)
    low = (rest - mid.astype(F32)).astype(BF)
    out = (jnp.dot(hi, ones, preferred_element_type=F32)
           + jnp.dot(mid, ones, preferred_element_type=F32)
           + jnp.dot(low, ones, preferred_element_type=F32))
    return jnp.concatenate([out[i:i + 1] for i in range(n)], axis=1)


def _normalized(a, count, width):
    ones = _groups(width)
    v = a.astype(F32)
    mean = _group_sum(jnp.sum(v, axis=0, keepdims=True), ones) * (1.0 / count)
    cen = v - mean
    var = _group_sum(jnp.sum(cen * cen, axis=0, keepdims=True), ones) * (1.0 / count)
    rstd = lax.rsqrt(var + EPSILON)
    return cen * rstd, rstd


def _gn_kernel(width, a_ref, gain_ref, bias_ref, h_ref):
    xhat, _ = _normalized(a_ref[...], PIX * width, width)
    n = xhat * gain_ref[...] + bias_ref[...]
    h_ref[...] = (n * jax.nn.sigmoid(n)).astype(BF)


def _prep_kernel(width, a_ref, gain_ref, bias_ref, h_ref, xhat_ref, slope_ref, rstd_ref):
    xhat, rstd = _normalized(a_ref[...], PIX * width, width)
    n = xhat * gain_ref[...] + bias_ref[...]
    s = jax.nn.sigmoid(n)
    h_ref[...] = (n * s).astype(BF)
    xhat_ref[...] = xhat
    slope_ref[...] = s * (1.0 + n * (1.0 - s))
    rstd_ref[...] = rstd


def _gn_bwd_kernel(width, dy_ref, own_ref, oth_ref, xhat_ref, slope_ref, rstd_ref, gain_ref,
                   da_ref, dg_ref, db_ref):
    ones = _groups(width)
    count = PIX * width
    dn = (own_ref[...] + oth_ref[...].astype(F32)) * slope_ref[...]
    xhat = xhat_ref[...]
    gain = gain_ref[...]
    db = jnp.sum(dn, axis=0, keepdims=True)
    dg = jnp.sum(dn * xhat, axis=0, keepdims=True)
    m1 = _group_sum(db * gain, ones) * (1.0 / count)
    m2 = _group_sum(dg * gain, ones) * (1.0 / count)
    da = dy_ref[...].astype(F32) + rstd_ref[...] * (dn * gain - m1 - xhat * m2)
    da_ref[...] = da.astype(BF)
    dg_ref[...] = dg
    db_ref[...] = db


def _pad_into(ref, value):
    zero = jnp.zeros((SIDE, ref.shape[1]), ref.dtype)
    ref[0:SIDE, :] = zero
    ref[SIDE:SIDE + PIX, :] = value
    ref[SIDE + PIX:, :] = zero


def _join_shifts(left, mid, right):
    x = lax.broadcasted_iota(jnp.int32, mid.shape, 0) % SIDE
    out = mid + jnp.where(x > 0, pltpu.roll(left, 1, 0), 0.0)
    return out + jnp.where(x < SIDE - 1, pltpu.roll(right, PIX - 1, 0), 0.0)


def _conv_kernel(own_ref, oth_ref, a_ref, w_ref, y_ref, hp_ref, hq_ref, acc_ref):
    t = pl.program_id(0)

    @pl.when(t == 0)
    def _():
        _pad_into(hp_ref, own_ref[...])
        _pad_into(hq_ref, oth_ref[...])

    ky = t // 3
    kx = t % 3
    half = own_ref.shape[1]
    row = pl.multiple_of(ky * SIDE, SIDE)
    part = (jnp.dot(hp_ref[pl.ds(row, PIX), :], w_ref[0, :half, :], preferred_element_type=F32)
            + jnp.dot(hq_ref[pl.ds(row, PIX), :], w_ref[0, half:, :], preferred_element_type=F32))

    @pl.when(ky == 0)
    def _():
        acc_ref[kx] = part

    @pl.when(ky > 0)
    def _():
        acc_ref[kx] += part

    @pl.when(t == 8)
    def _():
        z = _join_shifts(acc_ref[0], acc_ref[1], acc_ref[2])
        y_ref[...] = (a_ref[...].astype(F32) + z).astype(BF)


def _dgrad_kernel(dy_ref, w_ref, own_ref, oth_ref, dp_ref, acc_ref):
    t = pl.program_id(0)

    @pl.when(t == 0)
    def _():
        _pad_into(dp_ref, dy_ref[...])

    ky = t // 3
    kx = t % 3
    half = dy_ref.shape[1]
    row = pl.multiple_of((2 - ky) * SIDE, SIDE)
    part = lax.dot_general(dp_ref[pl.ds(row, PIX), :], w_ref[0], (((1,), (1,)), ((), ())),
                           preferred_element_type=F32)

    @pl.when(ky == 0)
    def _():
        acc_ref[kx] = part

    @pl.when(ky > 0)
    def _():
        acc_ref[kx] += part

    @pl.when(t == 8)
    def _():
        p = _join_shifts(acc_ref[2], acc_ref[1], acc_ref[0])
        own_ref[...] = p[:, :half]
        oth_ref[...] = p[:, half:].astype(BF)


def _dw_kernel(ht_ref, dy_ref, out_ref, pad_ref, rhs_ref):
    step = pl.program_id(0)
    count = dy_ref.shape[0]
    x = lax.broadcasted_iota(jnp.int32, (PIX, 128), 0) % SIDE
    for i in range(count):
        v = dy_ref[i].astype(F32)
        moved = (jnp.where(x < SIDE - 1, pltpu.roll(v, PIX - 1, 0), 0.0), v,
                 jnp.where(x > 0, pltpu.roll(v, 1, 0), 0.0))
        for kx in range(3):
            _pad_into(pad_ref.at[kx], moved[kx].astype(BF))
        for t in range(9):
            start = (2 - t // 3) * SIDE
            rhs_ref[i * PIX:(i + 1) * PIX, t * 128:(t + 1) * 128] = pad_ref[t % 3, start:start + PIX, :]

    for lo, taps in ((0, 2), (2, 2), (4, 2), (6, 2), (8, 1)):
        part = jnp.dot(ht_ref[...], rhs_ref[:, lo * 128:(lo + taps) * 128], preferred_element_type=F32)
        for i in range(taps):
            piece = part[:, i * 128:(i + 1) * 128]

            @pl.when(step == 0)
            def _():
                out_ref[lo + i] = piece

            @pl.when(step > 0)
            def _():
                out_ref[lo + i] += piece


def _assemble_kernel(idx_ref, w0, w1, w2, w3, out_ref, sem):
    copies = []
    for r, src in enumerate((w0, w1, w2, w3)):
        for z in range(4):
            for side in range(2):
                copies.append(pltpu.make_async_copy(
                    src.at[z, :, side],
                    out_ref.at[:, idx_ref[4 + side], idx_ref[r], :, pl.ds(z * 128, 128)],
                    sem.at[(r * 4 + z) * 2 + side]))
    for c in copies:
        c.start()
    for c in copies:
        c.wait()


def local(x_input, d_output, weights, gains, biases):
    row = lax.axis_index("dp")
    segment = lax.axis_index("segment")
    chan = lax.axis_index("chan")
    core = chan % 2
    width = weights.shape[2] // GROUPS
    half = 4 * 128
    ZG = [[0, 2, 4, 6], [1, 3, 5, 7]]
    axes = ("dp", "segment", "chan")

    def lin(d, s, k):
        return (d * 8 + s) * 8 + k

    def move(value, source, target):
        flip = (source < 4) != (target < 4)
        pairs = [(lin(d, source, k), lin(d, target, (6 - k + 2 * (k % 2)) if flip else k))
                 for d in range(4) for k in range(8)]
        return lax.ppermute(value, axes, pairs)

    def swap(value, seg):
        pairs = [(lin(d, seg, k), lin(d, seg, k ^ 1)) for d in range(4) for k in range(8)]
        return lax.ppermute(value, axes, pairs)

    def swap_all(value):
        return lax.ppermute(value, "chan", [(k, k ^ 1) for k in range(8)])

    def turn(value, by):
        return lax.ppermute(value, "dp", [(i, (i + by) % 4) for i in range(4)])

    def scatter_z(value):
        return lax.all_to_all(value, "chan", 0, 0, axis_index_groups=ZG, tiled=True)

    def flat(blocks):
        return jnp.transpose(blocks, (1, 0, 2)).reshape(PIX, half)

    def unflat(value):
        return jnp.transpose(value.reshape(PIX, 4, 128), (1, 0, 2))

    quarter = lax.dynamic_slice_in_dim(weights[0], row * 256, 256, 1)
    wz = scatter_z(jnp.broadcast_to(quarter[None], (4,) + quarter.shape))
    below = turn(wz, 1)
    above = turn(wz, -1)
    across = jnp.concatenate([turn(below[:2], 1), turn(above[2:], -1)], axis=0)
    pieces = [p.reshape(4, 9, 2, 128, 128) for p in (wz, above, across, below)]
    places = jnp.concatenate([(row + jnp.arange(4)) % 4, (core + jnp.arange(2)) % 2]).astype(jnp.int32)
    anyspec = pl.BlockSpec(memory_space=pl.ANY)
    w = pl.pallas_call(
        _assemble_kernel,
        out_shape=jax.ShapeDtypeStruct((9, 2, 4, 128, half), BF),
        grid_spec=pltpu.PrefetchScalarGridSpec(
            num_scalar_prefetch=1, grid=(), in_specs=[anyspec] * 4, out_specs=anyspec,
            scratch_shapes=[pltpu.SemaphoreType.DMA((32,))]),
        name="assemble",
    )(places, *pieces).reshape(9, 2 * half, half)

    rows = jnp.concatenate([gains, biases], axis=0)
    rows = scatter_z(jnp.broadcast_to(rows[None], (4, 2, 128)))
    rows = jnp.transpose(rows, (1, 0, 2)).reshape(2, half)
    gain = rows[0:1]
    bias = rows[1:2]

    act = jax.ShapeDtypeStruct((PIX, half), BF)
    act32 = jax.ShapeDtypeStruct((PIX, half), F32)
    line = jax.ShapeDtypeStruct((1, half), F32)

    def normed(a):
        return pl.pallas_call(lambda *r: _gn_kernel(width, *r), out_shape=act, name="gn")(a, gain, bias)

    def prep(a):
        return pl.pallas_call(lambda *r: _prep_kernel(width, *r), out_shape=(act, act32, act32, line),
                              name="prep")(a, gain, bias)

    full = pl.BlockSpec((PIX, half), lambda t: (0, 0))
    wspec = pl.BlockSpec((1, 2 * half, half), lambda t: (t, 0, 0))

    def conv(own, oth, a):
        return pl.pallas_call(
            _conv_kernel, grid=(9,), in_specs=[full, full, full, wspec], out_specs=full, out_shape=act,
            scratch_shapes=[pltpu.VMEM((PIX + 2 * SIDE, half), BF), pltpu.VMEM((PIX + 2 * SIDE, half), BF),
                            pltpu.VMEM((3, PIX, half), F32)],
            name="conv")(own, oth, a, w)

    def dgrad(dy):
        return pl.pallas_call(
            _dgrad_kernel, grid=(9,), in_specs=[full, wspec], out_specs=(full, full), out_shape=(act32, act),
            scratch_shapes=[pltpu.VMEM((PIX + 2 * SIDE, half), BF), pltpu.VMEM((3, PIX, 2 * half), F32)],
            name="dgrad")(dy, w)

    def added(p, q):
        return (p.astype(F32) + q.astype(F32)).astype(BF)

    first = flat(scatter_z(x_input[:, 0]))
    a = jnp.where(segment == 0, first, jnp.zeros_like(first))
    inputs = [a]
    skips = {}
    for j in range(7):
        own = normed(a)
        y = conv(own, swap(own, j), a)
        if j < 3:
            skips[j] = move(y, j, 7 - j)
        a = move(y, j, j + 1)
        if j >= 4:
            a = added(a, skips[6 - j])
        inputs.append(a)
    mine = inputs[0]
    for a in inputs[1:]:
        mine = mine + a

    hidden, xhat, slope, rstd = prep(mine)

    last = flat(scatter_z(d_output[::-1, 0]))
    dy = jnp.where(segment == 7, last, jnp.zeros_like(last))
    grads = []
    gain_sum = bias_sum = 0.0
    skip_grads = {}
    h_turned = None
    for j in reversed(range(8)):
        if j == 3:
            hidden, dy = lax.optimization_barrier((hidden, dy))
            hz = scatter_z(jnp.broadcast_to(hidden[None], (4, PIX, half)))
            hall = jnp.concatenate([hz, turn(hz, -1), turn(hz, 2), turn(hz, 1)], axis=0)
            hoth = swap_all(hall)
            pair = jnp.stack([jnp.where(core == 0, hall, hoth), jnp.where(core == 0, hoth, hall)])
            pair = pair.reshape(2, 16 * PIX, 4, 128)
            h_turned = jnp.transpose(pair, (2, 0, 3, 1)).reshape(2 * half, 16 * PIX)
            h_turned, dy = lax.optimization_barrier((h_turned, dy))
        grads.append(dy)
        own, oth = dgrad(dy)
        da, dg, db = pl.pallas_call(
            lambda *r: _gn_bwd_kernel(width, *r), out_shape=(act, line, line), name="gn_bwd",
        )(dy, own, swap(oth, j), xhat, slope, rstd, gain)
        gain_sum = gain_sum + dg
        bias_sum = bias_sum + db
        if j > 4:
            skip_grads[7 - j] = move(da, j, 7 - j)
        if j > 0:
            dy = move(da, j, j - 1)
            if j - 1 < 3:
                dy = added(dy, skip_grads[j - 1])

    mine = grads[0]
    for g in grads[1:]:
        mine = mine + g
    dz = scatter_z(unflat(mine))
    dall = jnp.concatenate([dz, turn(dz, -1), turn(dz, 2), turn(dz, 1)], axis=0)
    grad_weight = pl.pallas_call(
        _dw_kernel, grid=(4,),
        in_specs=[pl.BlockSpec((2 * half, 4 * PIX), lambda i: (0, i)),
                  pl.BlockSpec((4, PIX, 128), lambda i: (i, 0, 0))],
        out_specs=pl.BlockSpec((9, 2 * half, 128), lambda i: (0, 0, 0)),
        out_shape=jax.ShapeDtypeStruct((9, 2 * half, 128), F32),
        scratch_shapes=[pltpu.VMEM((3, PIX + 2 * SIDE, 128), BF), pltpu.VMEM((4 * PIX, 9 * 128), BF)],
        name="dw")(h_turned, dall)

    small = jnp.concatenate([gain_sum, bias_sum], axis=0).reshape(2, 4, 128)
    small = jnp.sum(scatter_z(jnp.transpose(small, (1, 0, 2))), axis=0)
    small = lax.psum(small, "dp")
    return (grad_weight[None], small[0:1], small[1:2])


def solution(mesh):
    in_specs = (
        P(None, "dp", None, "chan"),
        P(None, "dp", None, "chan"),
        P("segment", None, None, "chan"),
        P("segment", "chan"),
        P("segment", "chan"),
    )
    out_specs = (P("segment", None, None, "chan"), P("segment", "chan"), P("segment", "chan"))
    return jax.shard_map(local, mesh=mesh, in_specs=in_specs, out_specs=out_specs, check_vma=False)
```

```python
import jax
import jax.numpy as jnp
from jax import lax
from jax.experimental import pallas as pl
from jax.experimental.pallas import tpu as pltpu
from jax.sharding import PartitionSpec as P


GROUPS = 32
SIDE = 16
EPSILON = 1e-05
PIX = SIDE * SIDE
BF = jnp.bfloat16
F32 = jnp.float32


def _groups(width):
    r = lax.broadcasted_iota(jnp.int32, (128, 128), 0) // width
    c = lax.broadcasted_iota(jnp.int32, (128, 128), 1) // width
    return jnp.where(r == c, 1.0, 0.0).astype(BF)


def _group_sum(v, ones):
    n = v.shape[1] // 128
    rows = jnp.concatenate([v[:, i * 128:(i + 1) * 128] for i in range(n)], axis=0)
    hi = rows.astype(BF)
    rest = rows - hi.astype(F32)
    mid = rest.astype(BF)
    low = (rest - mid.astype(F32)).astype(BF)
    out = (jnp.dot(hi, ones, preferred_element_type=F32)
           + jnp.dot(mid, ones, preferred_element_type=F32)
           + jnp.dot(low, ones, preferred_element_type=F32))
    return jnp.concatenate([out[i:i + 1] for i in range(n)], axis=1)


def _normalized(a, count, width):
    ones = _groups(width)
    v = a.astype(F32)
    mean = _group_sum(jnp.sum(v, axis=0, keepdims=True), ones) * (1.0 / count)
    cen = v - mean
    var = _group_sum(jnp.sum(cen * cen, axis=0, keepdims=True), ones) * (1.0 / count)
    rstd = lax.rsqrt(var + EPSILON)
    return cen * rstd, rstd


def _gn_kernel(width, a_ref, gain_ref, bias_ref, h_ref):
    xhat, _ = _normalized(a_ref[...], PIX * width, width)
    n = xhat * gain_ref[...] + bias_ref[...]
    h_ref[...] = (n * jax.nn.sigmoid(n)).astype(BF)


def _prep_kernel(width, a_ref, gain_ref, bias_ref, h_ref, xhat_ref, slope_ref, rstd_ref):
    xhat, rstd = _normalized(a_ref[...], PIX * width, width)
    n = xhat * gain_ref[...] + bias_ref[...]
    s = jax.nn.sigmoid(n)
    h_ref[...] = (n * s).astype(BF)
    xhat_ref[...] = xhat
    slope_ref[...] = s * (1.0 + n * (1.0 - s))
    rstd_ref[...] = rstd


def _gn_bwd_kernel(width, dy_ref, own_ref, oth_ref, xhat_ref, slope_ref, rstd_ref, gain_ref,
                   da_ref, dg_ref, db_ref):
    ones = _groups(width)
    count = PIX * width
    dn = (own_ref[...] + oth_ref[...].astype(F32)) * slope_ref[...]
    xhat = xhat_ref[...]
    gain = gain_ref[...]
    db = jnp.sum(dn, axis=0, keepdims=True)
    dg = jnp.sum(dn * xhat, axis=0, keepdims=True)
    m1 = _group_sum(db * gain, ones) * (1.0 / count)
    m2 = _group_sum(dg * gain, ones) * (1.0 / count)
    da = dy_ref[...].astype(F32) + rstd_ref[...] * (dn * gain - m1 - xhat * m2)
    da_ref[...] = da.astype(BF)
    dg_ref[...] = dg
    db_ref[...] = db


def _pad_into(ref, value):
    zero = jnp.zeros((SIDE, ref.shape[1]), ref.dtype)
    ref[0:SIDE, :] = zero
    ref[SIDE:SIDE + PIX, :] = value
    ref[SIDE + PIX:, :] = zero


def _join_shifts(left, mid, right):
    x = lax.broadcasted_iota(jnp.int32, mid.shape, 0) % SIDE
    out = mid + jnp.where(x > 0, pltpu.roll(left, 1, 0), 0.0)
    return out + jnp.where(x < SIDE - 1, pltpu.roll(right, PIX - 1, 0), 0.0)


def _cat_into(ref, col, value, turn):
    wide = value.shape[1]
    zero = jnp.zeros((SIDE, wide), value.dtype)
    for ky in range(3):
        lo = ky * (ref.shape[1] // 3) + col
        by = (ky - 1) * turn
        if by == 0:
            ref[:, lo:lo + wide] = value
        elif by < 0:
            ref[0:SIDE, lo:lo + wide] = zero
            ref[SIDE:, lo:lo + wide] = value[:PIX - SIDE]
        else:
            ref[0:PIX - SIDE, lo:lo + wide] = value[SIDE:]
            ref[PIX - SIDE:, lo:lo + wide] = zero


def _conv_kernel(own_ref, oth_ref, a_ref, w_ref, y_ref, cat_ref, acc_ref):
    kx = pl.program_id(0)

    @pl.when(kx == 0)
    def _():
        _cat_into(cat_ref, 0, own_ref[...], 1)
        _cat_into(cat_ref, own_ref.shape[1], oth_ref[...], 1)

    acc_ref[kx] = jnp.dot(cat_ref[...], w_ref[0], preferred_element_type=F32)

    @pl.when(kx == 2)
    def _():
        z = _join_shifts(acc_ref[0], acc_ref[1], acc_ref[2])
        y_ref[...] = (a_ref[...].astype(F32) + z).astype(BF)


def _dgrad_kernel(dy_ref, w_ref, own_ref, oth_ref, cat_ref, acc_ref):
    kx = pl.program_id(0)

    @pl.when(kx == 0)
    def _():
        _cat_into(cat_ref, 0, dy_ref[...], -1)

    acc_ref[kx] = jnp.dot(cat_ref[...], w_ref[0], preferred_element_type=F32)

    @pl.when(kx == 2)
    def _():
        half = dy_ref.shape[1]
        p = _join_shifts(acc_ref[2], acc_ref[1], acc_ref[0])
        own_ref[...] = p[:, :half]
        oth_ref[...] = p[:, half:].astype(BF)


def _dw_kernel(idx_ref, own_ref, oth_ref, dy_ref, out_ref, pad_ref, rhs_ref):
    @pl.when(pl.program_id(0) == 0)
    def _():
        x = lax.broadcasted_iota(jnp.int32, (PIX, 128), 0) % SIDE

        def build(i, carry):
            v = dy_ref[i].astype(F32)
            moved = (jnp.where(x < SIDE - 1, pltpu.roll(v, PIX - 1, 0), 0.0), v,
                     jnp.where(x > 0, pltpu.roll(v, 1, 0), 0.0))
            for kx in range(3):
                _pad_into(pad_ref.at[kx], moved[kx].astype(BF))
            for t in range(9):
                start = (2 - t // 3) * SIDE
                rhs_ref[pl.ds(pl.multiple_of(i * PIX, PIX), PIX), t * 128:(t + 1) * 128] = (
                    pad_ref[t % 3, start:start + PIX, :])
            return carry

        lax.fori_loop(0, dy_ref.shape[0], build, 0)

    h = jnp.concatenate([own_ref[...], oth_ref[...]], axis=1)
    for lo, taps in ((0, 2), (2, 2), (4, 2), (6, 2), (8, 1)):
        part = lax.dot_general(h, rhs_ref[:, lo * 128:(lo + taps) * 128], (((0,), (0,)), ((), ())),
                               preferred_element_type=F32)
        for i in range(taps):
            for side in range(2):
                at = pl.multiple_of(idx_ref[side] * 128, 128)
                out_ref[lo + i, pl.ds(at, 128), :] = part[side * 128:(side + 1) * 128, i * 128:(i + 1) * 128]


def _assemble_kernel(idx_ref, *refs):
    out_ref = refs[-1]
    for r in range(4):
        for side in range(2):
            for kx in range(3):
                out_ref[kx, 0, idx_ref[4 + side], idx_ref[r]] = refs[r][kx, side]


def local(x_input, d_output, weights, gains, biases):
    row = lax.axis_index("dp")
    segment = lax.axis_index("segment")
    chan = lax.axis_index("chan")
    z = chan // 2
    core = chan % 2
    width = weights.shape[2] // GROUPS
    half = 4 * 128
    axes = ("dp", "segment", "chan")

    def lin(d, s, k):
        return (d * 8 + s) * 8 + k

    def move(value, source, target):
        flip = (source < 4) != (target < 4)
        pairs = [(lin(d, source, k), lin(d, target, (6 - k + 2 * (k % 2)) if flip else k))
                 for d in range(4) for k in range(8)]
        return lax.ppermute(value, axes, pairs)

    def swap(value):
        return lax.ppermute(value, "chan", [(k, k ^ 1) for k in range(8)])

    def turn(value, by):
        return lax.ppermute(value, "dp", [(i, (i + by) % 4) for i in range(4)])

    def turn_z(value, by):
        return lax.ppermute(value, "chan", [(k, (k + 2 * by) % 8) for k in range(8)])

    def ordered(parts):
        turn_of = [parts[0], parts[3], parts[2], parts[1]]
        return lax.dynamic_slice_in_dim(jnp.concatenate(turn_of * 2, axis=1), (4 - z) % 4 * 128, half, 1)

    def spread(pick):
        return ordered([pick(z)] + [turn_z(pick((z + by) % 4), by) for by in (1, 2, 3)])

    quarter = lax.dynamic_slice_in_dim(weights[0], row * 256, 256, 1)
    sides = [(row + jnp.arange(4)) % 4, (core + jnp.arange(2)) % 2]
    w = None
    token = None
    pieces = {}
    for by in (0, 1, 3, 2):
        piece = quarter
        if by > 1:
            piece, token = lax.optimization_barrier((piece, token))
        if by > 0:
            piece = turn_z(piece, by)
        token = piece
        below = turn(piece, 1)
        above = turn(piece, -1)
        across = jnp.concatenate([turn(below[:5], 1), turn(above[5:], -1)], axis=0)
        pieces[by] = [p.reshape(9, 2, 128, 128) for p in (piece, above, across, below)]
    for by in (0, 1, 3, 2):
        places = jnp.concatenate(sides + [(z - by)[None] % 4]).astype(jnp.int32)
        w = pl.pallas_call(
            _assemble_kernel,
            out_shape=jax.ShapeDtypeStruct((3, 3, 2, 4, 128, half), BF),
            grid_spec=pltpu.PrefetchScalarGridSpec(
                num_scalar_prefetch=1, grid=(3,),
                in_specs=[pl.BlockSpec((3, 2, 128, 128), lambda t, i: (t, 0, 0, 0))] * 4
                + ([] if w is None else [pl.BlockSpec(memory_space=pl.ANY)]),
                out_specs=pl.BlockSpec((3, 1, 2, 4, 128, 128), lambda t, i: (0, t, 0, 0, 0, i[6]))),
            input_output_aliases={} if w is None else {5: 0},
            name="assemble",
        )(places, *pieces[by], *([] if w is None else [w]))
    w = w.reshape(3, 6 * half, half)

    rows = jnp.concatenate([gains, biases], axis=0)
    rows = spread(lambda t: rows)
    gain = rows[0:1]
    bias = rows[1:2]

    act = jax.ShapeDtypeStruct((PIX, half), BF)
    act32 = jax.ShapeDtypeStruct((PIX, half), F32)
    line = jax.ShapeDtypeStruct((1, half), F32)

    def normed(a):
        return pl.pallas_call(lambda *r: _gn_kernel(width, *r), out_shape=act, name="gn")(a, gain, bias)

    def prep(a):
        return pl.pallas_call(lambda *r: _prep_kernel(width, *r), out_shape=(act, act32, act32, line),
                              name="prep")(a, gain, bias)

    full = pl.BlockSpec((PIX, half), lambda t: (0, 0))

    def conv(own, oth, a):
        return pl.pallas_call(
            _conv_kernel, grid=(3,),
            in_specs=[full, full, full, pl.BlockSpec((1, 6 * half, half), lambda t: (t, 0, 0))],
            out_specs=full, out_shape=act,
            scratch_shapes=[pltpu.VMEM((PIX, 6 * half), BF), pltpu.VMEM((3, PIX, half), F32)],
            name="conv")(own, oth, a, w)

    def dgrad(dy):
        return pl.pallas_call(
            _dgrad_kernel, grid=(3,),
            in_specs=[full, pl.BlockSpec((1, 3 * half, 2 * half), lambda t: (t, 0, 0))],
            out_specs=(full, full), out_shape=(act32, act),
            scratch_shapes=[pltpu.VMEM((PIX, 3 * half), BF), pltpu.VMEM((3, PIX, 2 * half), F32)],
            name="dgrad")(dy, w_turned)

    def added(p, q):
        return (p.astype(F32) + q.astype(F32)).astype(BF)

    first = spread(lambda t: lax.dynamic_index_in_dim(x_input[:, 0], t, 0, keepdims=False))
    last = spread(lambda t: lax.dynamic_index_in_dim(d_output[:, 0], 3 - t, 0, keepdims=False))
    first, last, gain, bias, w = lax.optimization_barrier((first, last, gain, bias, w))
    a = jnp.where(segment == 0, first, jnp.zeros_like(first))
    inputs = [a]
    skips = {}
    for j in range(7):
        own = normed(a)
        oth = swap(own)
        y = conv(own, oth, a)
        if j == 3:
            late, y = lax.optimization_barrier((w, y))
        a = move(y, j, j + 1)
        if j < 3:
            skips[j] = move(y, j, 7 - j)
        if j >= 4:
            a = added(a, skips[6 - j])
        inputs.append(a)
    mine = inputs[0]
    for a in inputs[1:]:
        mine = mine + a

    hidden, xhat, slope, rstd = prep(mine)
    w_turned = jnp.transpose(late.reshape(3, 3, 2 * half, half), (0, 1, 3, 2)).reshape(3, 3 * half, 2 * half)

    dy = jnp.where(segment == 7, last, jnp.zeros_like(last))
    grads = []
    gain_sum = bias_sum = 0.0
    skip_grads = {}
    for j in reversed(range(8)):
        if j == 3:
            own_all, oth_all, dy = lax.optimization_barrier((own_all, oth_all, dy))
        if j == 0:
            mine = grads[0]
            for g in grads[1:]:
                mine = mine + g
            mine = mine + dy
            dz = [lax.dynamic_slice_in_dim(mine, (z + by) % 4 * 128, 128, 1) for by in range(4)]
            dz = jnp.stack(dz[:1] + [turn_z(dz[by], by) for by in (1, 2, 3)])
            dz, dy = lax.optimization_barrier((dz, dy))
            turned = [turn(dz, -1), turn(dz, 2), turn(dz, 1)]
            dall = jnp.concatenate([dz] + turned, axis=0)
        grads.append(dy)
        own, oth = dgrad(dy)
        oth = swap(oth)
        da, dg, db = pl.pallas_call(
            lambda *r: _gn_bwd_kernel(width, *r), out_shape=(act, line, line), name="gn_bwd",
        )(dy, own, oth, xhat, slope, rstd, gain)
        gain_sum = gain_sum + dg
        bias_sum = bias_sum + db
        if j > 0:
            dy = move(da, j, j - 1)
        if j > 4:
            skip_grads[7 - j] = move(da, j, 7 - j)
        if 0 < j < 4:
            dy = added(dy, skip_grads[j - 1])
        if j == 4:
            hidden, dg = lax.optimization_barrier((hidden, dg))
            hz = jnp.stack([hidden] + [turn_z(hidden, by) for by in (1, 2, 3)])
            own_all = jnp.concatenate([hz, turn(hz, -1), turn(hz, 2), turn(hz, 1)], axis=0)
            oth_all = swap(own_all)

    flip = jnp.stack([core, 1 - core]).astype(jnp.int32)
    hspec = pl.BlockSpec((16 * PIX, 128), lambda i, c: (0, i))
    grad_weight = pl.pallas_call(
        _dw_kernel,
        out_shape=jax.ShapeDtypeStruct((9, 2 * half, 128), F32),
        grid_spec=pltpu.PrefetchScalarGridSpec(
            num_scalar_prefetch=1, grid=(4,),
            in_specs=[hspec, hspec, pl.BlockSpec((16, PIX, 128), lambda i, c: (0, 0, 0))],
            out_specs=pl.BlockSpec((9, 256, 128), lambda i, c: (0, i, 0)),
            scratch_shapes=[pltpu.VMEM((3, PIX + 2 * SIDE, 128), BF), pltpu.VMEM((16 * PIX, 9 * 128), BF)]),
        name="dw")(flip, own_all.reshape(16 * PIX, half), oth_all.reshape(16 * PIX, half), dall)

    small = jnp.transpose(jnp.concatenate([gain_sum, bias_sum], axis=0).reshape(2, 4, 128), (1, 0, 2))
    total = lax.dynamic_index_in_dim(small, z, 0, keepdims=False)
    for by in (1, 2, 3):
        piece = lax.dynamic_index_in_dim(small, (z + by) % 4, 0, keepdims=False)
        total = total + turn_z(piece, by)
    small = total + turn(total, 1) + turn(total, 2) + turn(total, -1)
    return (grad_weight[None], small[0:1], small[1:2])


def solution(mesh):
    in_specs = (
        P(None, "dp", None, "chan"),
        P(None, "dp", None, "chan"),
        P("segment", None, None, "chan"),
        P("segment", "chan"),
        P("segment", "chan"),
    )
    out_specs = (P("segment", None, None, "chan"), P("segment", "chan"), P("segment", "chan"))

    return jax.shard_map(local, mesh=mesh, in_specs=in_specs, out_specs=out_specs, check_vma=False)
```

```python
import jax
import jax.numpy as jnp
from jax import lax
from jax.experimental import pallas as pl
from jax.experimental.pallas import tpu as pltpu
from jax.sharding import PartitionSpec as P


GROUPS = 32
SIDE = 16
EPSILON = 1e-05
PIX = SIDE * SIDE
BF = jnp.bfloat16
F32 = jnp.float32


def _groups(width):
    r = lax.broadcasted_iota(jnp.int32, (128, 128), 0) // width
    c = lax.broadcasted_iota(jnp.int32, (128, 128), 1) // width
    return jnp.where(r == c, 1.0, 0.0).astype(BF)


def _group_sum(v, ones):
    n = v.shape[1] // 128
    rows = jnp.concatenate([v[:, i * 128:(i + 1) * 128] for i in range(n)], axis=0)
    hi = rows.astype(BF)
    rest = rows - hi.astype(F32)
    mid = rest.astype(BF)
    low = (rest - mid.astype(F32)).astype(BF)
    out = (jnp.dot(hi, ones, preferred_element_type=F32)
           + jnp.dot(mid, ones, preferred_element_type=F32)
           + jnp.dot(low, ones, preferred_element_type=F32))
    return jnp.concatenate([out[i:i + 1] for i in range(n)], axis=1)


def _normalized(a, count, width):
    ones = _groups(width)
    v = a.astype(F32)
    mean = _group_sum(jnp.sum(v, axis=0, keepdims=True), ones) * (1.0 / count)
    cen = v - mean
    var = _group_sum(jnp.sum(cen * cen, axis=0, keepdims=True), ones) * (1.0 / count)
    rstd = lax.rsqrt(var + EPSILON)
    return cen * rstd, rstd


def _gn_kernel(width, a_ref, gain_ref, bias_ref, h_ref):
    xhat, _ = _normalized(a_ref[...], PIX * width, width)
    n = xhat * gain_ref[...] + bias_ref[...]
    h_ref[...] = (n * jax.nn.sigmoid(n)).astype(BF)


def _prep_kernel(width, a_ref, gain_ref, bias_ref, h_ref, xhat_ref, slope_ref, rstd_ref):
    xhat, rstd = _normalized(a_ref[...], PIX * width, width)
    n = xhat * gain_ref[...] + bias_ref[...]
    s = jax.nn.sigmoid(n)
    h_ref[...] = (n * s).astype(BF)
    xhat_ref[...] = xhat
    slope_ref[...] = s * (1.0 + n * (1.0 - s))
    rstd_ref[...] = rstd


def _gn_bwd_kernel(width, dy_ref, own_ref, oth_ref, xhat_ref, slope_ref, rstd_ref, gain_ref,
                   da_ref, dg_ref, db_ref):
    ones = _groups(width)
    count = PIX * width
    dn = (own_ref[...] + oth_ref[...].astype(F32)) * slope_ref[...]
    xhat = xhat_ref[...]
    gain = gain_ref[...]
    db = jnp.sum(dn, axis=0, keepdims=True)
    dg = jnp.sum(dn * xhat, axis=0, keepdims=True)
    m1 = _group_sum(db * gain, ones) * (1.0 / count)
    m2 = _group_sum(dg * gain, ones) * (1.0 / count)
    da = dy_ref[...].astype(F32) + rstd_ref[...] * (dn * gain - m1 - xhat * m2)
    da_ref[...] = da.astype(BF)
    dg_ref[...] = dg
    db_ref[...] = db


def _pad_into(ref, value):
    zero = jnp.zeros((SIDE, ref.shape[1]), ref.dtype)
    ref[0:SIDE, :] = zero
    ref[SIDE:SIDE + PIX, :] = value
    ref[SIDE + PIX:, :] = zero


def _join_shifts(left, mid, right):
    x = lax.broadcasted_iota(jnp.int32, mid.shape, 0) % SIDE
    out = mid + jnp.where(x > 0, pltpu.roll(left, 1, 0), 0.0)
    return out + jnp.where(x < SIDE - 1, pltpu.roll(right, PIX - 1, 0), 0.0)


def _cat_into(ref, col, value, turn):
    wide = value.shape[1]
    zero = jnp.zeros((SIDE, wide), value.dtype)
    for ky in range(3):
        lo = ky * (ref.shape[1] // 3) + col
        by = (ky - 1) * turn
        if by == 0:
            ref[:, lo:lo + wide] = value
        elif by < 0:
            ref[0:SIDE, lo:lo + wide] = zero
            ref[SIDE:, lo:lo + wide] = value[:PIX - SIDE]
        else:
            ref[0:PIX - SIDE, lo:lo + wide] = value[SIDE:]
            ref[PIX - SIDE:, lo:lo + wide] = zero


def _conv_kernel(on_ref, own_ref, oth_ref, a_ref, w_ref, y_ref, cat_ref, acc_ref):
    kx = pl.program_id(0)

    @pl.when(on_ref[0] > 0)
    def _():
        _conv_step(kx, own_ref, oth_ref, a_ref, w_ref, y_ref, cat_ref, acc_ref)

    @pl.when((on_ref[0] == 0) & (kx == 0))
    def _():
        y_ref[...] = jnp.zeros_like(y_ref)


def _conv_step(kx, own_ref, oth_ref, a_ref, w_ref, y_ref, cat_ref, acc_ref):

    @pl.when(kx == 0)
    def _():
        _cat_into(cat_ref, 0, own_ref[...], 1)
        _cat_into(cat_ref, own_ref.shape[1], oth_ref[...], 1)

    acc_ref[kx] = jnp.dot(cat_ref[...], w_ref[0], preferred_element_type=F32)

    @pl.when(kx == 2)
    def _():
        z = _join_shifts(acc_ref[0], acc_ref[1], acc_ref[2])
        y_ref[...] = (a_ref[...].astype(F32) + z).astype(BF)


def _dgrad_kernel(on_ref, dy_ref, w_ref, own_ref, oth_ref, cat_ref, acc_ref):
    kx = pl.program_id(0)

    @pl.when(on_ref[0] > 0)
    def _():
        _dgrad_step(kx, dy_ref, w_ref, own_ref, oth_ref, cat_ref, acc_ref)

    @pl.when((on_ref[0] == 0) & (kx == 0))
    def _():
        own_ref[...] = jnp.zeros_like(own_ref)
        oth_ref[...] = jnp.zeros_like(oth_ref)


def _dgrad_step(kx, dy_ref, w_ref, own_ref, oth_ref, cat_ref, acc_ref):

    @pl.when(kx == 0)
    def _():
        _cat_into(cat_ref, 0, dy_ref[...], -1)

    acc_ref[kx] = jnp.dot(cat_ref[...], w_ref[0], preferred_element_type=F32)

    @pl.when(kx == 2)
    def _():
        half = dy_ref.shape[1]
        p = _join_shifts(acc_ref[2], acc_ref[1], acc_ref[0])
        own_ref[...] = p[:, :half]
        oth_ref[...] = p[:, half:].astype(BF)


def _dw_kernel(idx_ref, own_ref, oth_ref, dy_ref, out_ref, pad_ref, rhs_ref):
    @pl.when(pl.program_id(0) == 0)
    def _():
        x = lax.broadcasted_iota(jnp.int32, (PIX, 128), 0) % SIDE

        def build(i, carry):
            v = dy_ref[i].astype(F32)
            moved = (jnp.where(x < SIDE - 1, pltpu.roll(v, PIX - 1, 0), 0.0), v,
                     jnp.where(x > 0, pltpu.roll(v, 1, 0), 0.0))
            for kx in range(3):
                _pad_into(pad_ref.at[kx], moved[kx].astype(BF))
            for t in range(9):
                start = (2 - t // 3) * SIDE
                rhs_ref[pl.ds(pl.multiple_of(i * PIX, PIX), PIX), t * 128:(t + 1) * 128] = (
                    pad_ref[t % 3, start:start + PIX, :])
            return carry

        lax.fori_loop(0, dy_ref.shape[0], build, 0)

    h = jnp.concatenate([own_ref[...], oth_ref[...]], axis=1)
    for lo, taps in ((0, 2), (2, 2), (4, 2), (6, 2), (8, 1)):
        part = lax.dot_general(h, rhs_ref[:, lo * 128:(lo + taps) * 128], (((0,), (0,)), ((), ())),
                               preferred_element_type=F32)
        for i in range(taps):
            for side in range(2):
                at = pl.multiple_of(idx_ref[side] * 128, 128)
                out_ref[lo + i, pl.ds(at, 128), :] = part[side * 128:(side + 1) * 128, i * 128:(i + 1) * 128]


def _assemble_kernel(idx_ref, near, up, down, far0, far1, *rest):
    out_ref = rest[-1]
    for side in range(2):
        at = idx_ref[4 + side]
        for kx in range(3):
            out_ref[kx, 0, at, idx_ref[0]] = near[side, kx]
            out_ref[kx, 0, at, idx_ref[1]] = up[side, kx]
            out_ref[kx, 0, at, idx_ref[2]] = (far0, far1)[side][kx]
            out_ref[kx, 0, at, idx_ref[3]] = down[side, kx]


def _place_kernel(idx_ref, *refs):
    for by in range(4):
        refs[4][:, pl.ds(pl.multiple_of(idx_ref[by] * 128, 128), 128)] = refs[by][...]


def _limit(mib):
    return pltpu.CompilerParams(vmem_limit_bytes=mib << 20)


def local(x_input, d_output, weights, gains, biases):
    row = lax.axis_index("dp")
    segment = lax.axis_index("segment")
    chan = lax.axis_index("chan")
    z = chan // 2
    core = chan % 2
    width = weights.shape[2] // GROUPS
    half = 4 * 128
    axes = ("dp", "segment", "chan")

    def lin(d, s, k):
        return (d * 8 + s) * 8 + k

    def move(value, source, target):
        flip = (source < 4) != (target < 4)
        pairs = [(lin(d, source, k), lin(d, target, (6 - k + 2 * (k % 2)) if flip else k))
                 for d in range(4) for k in range(8)]
        return lax.ppermute(value, axes, pairs)

    def swap(value):
        return lax.ppermute(value, "chan", [(k, k ^ 1) for k in range(8)])

    def turn(value, by):
        return lax.ppermute(value, "dp", [(i, (i + by) % 4) for i in range(4)])

    def turn_z(value, by):
        return lax.ppermute(value, "chan", [(k, (k + 2 * by) % 8) for k in range(8)])

    sources = ((z - jnp.arange(4)) % 4).astype(jnp.int32)

    def send(pick):
        return [pick(z)] + [turn_z(pick((z + by) % 4), by) for by in (1, 2, 3)]

    def place(parts):
        shape = jax.ShapeDtypeStruct((parts[0].shape[0], half), parts[0].dtype)
        return pl.pallas_call(
            _place_kernel, out_shape=shape,
            grid_spec=pltpu.PrefetchScalarGridSpec(
                num_scalar_prefetch=1, grid=(1,),
                in_specs=[pl.BlockSpec(parts[0].shape, lambda t, i: (0, 0))] * 4,
                out_specs=pl.BlockSpec(shape.shape, lambda t, i: (0, 0))),
            compiler_params=_limit(6), name="place")(sources, *parts)

    rows = jnp.concatenate([gains, biases], axis=0)
    rows = send(lambda t: rows)
    first = send(lambda t: lax.dynamic_index_in_dim(x_input[:, 0], t, 0, keepdims=False))
    last = send(lambda t: lax.dynamic_index_in_dim(d_output[:, 0], 3 - t, 0, keepdims=False))

    quarter = lax.dynamic_slice_in_dim(weights[0], row * 256, 256, 1)
    quarter = jnp.transpose(quarter.reshape(9, 2, 128, 128), (1, 0, 2, 3))
    rows, first, last, quarter = lax.optimization_barrier((rows, first, last, quarter))
    sides = [(row + jnp.arange(4)) % 4, (core + jnp.arange(2)) % 2]
    w = None
    token = None
    pieces = {}
    for by in (0, 1, 3, 2):
        piece = quarter
        if by > 1:
            piece, token = lax.optimization_barrier((piece, token))
        if by > 0:
            piece = turn_z(piece, by)
        token = piece
        below = turn(piece, 1)
        above = turn(piece, -1)
        far = [turn(below[0], 1), turn(above[1], -1)]
        pieces[by] = [piece, above, below] + far
    for by in (0, 1, 3, 2):
        places = jnp.concatenate(sides + [(z - by)[None] % 4]).astype(jnp.int32)
        w = pl.pallas_call(
            _assemble_kernel,
            out_shape=jax.ShapeDtypeStruct((3, 3, 2, 4, 128, half), BF),
            grid_spec=pltpu.PrefetchScalarGridSpec(
                num_scalar_prefetch=1, grid=(3,),
                in_specs=[pl.BlockSpec((2, 3, 128, 128), lambda t, i: (0, t, 0, 0))] * 3
                + [pl.BlockSpec((3, 128, 128), lambda t, i: (t, 0, 0))] * 2
                + ([] if w is None else [pl.BlockSpec(memory_space=pl.ANY)]),
                out_specs=pl.BlockSpec((3, 1, 2, 4, 128, 128), lambda t, i: (0, t, 0, 0, 0, i[6]))),
            input_output_aliases={} if w is None else {6: 0},
            compiler_params=_limit(52), name="assemble",
        )(places, *pieces[by], *([] if w is None else [w]))
    w = w.reshape(3, 6 * half, half)

    rows = place(rows)
    gain = rows[0:1]
    bias = rows[1:2]

    act = jax.ShapeDtypeStruct((PIX, half), BF)
    act32 = jax.ShapeDtypeStruct((PIX, half), F32)
    line = jax.ShapeDtypeStruct((1, half), F32)

    def normed(a):
        return pl.pallas_call(lambda *r: _gn_kernel(width, *r), out_shape=act, compiler_params=_limit(6), name="gn")(a, gain, bias)

    def prep(a):
        return pl.pallas_call(lambda *r: _prep_kernel(width, *r), out_shape=(act, act32, act32, line),
                              compiler_params=_limit(10), name="prep")(a, gain, bias)

    full = pl.BlockSpec((PIX, half), lambda t, on: (0, 0))

    def turn_on(j):
        return jnp.where(segment == j, 1, 0).astype(jnp.int32).reshape(1)

    def conv(j, own, oth, a):
        return pl.pallas_call(
            _conv_kernel, out_shape=act,
            grid_spec=pltpu.PrefetchScalarGridSpec(
                num_scalar_prefetch=1, grid=(3,),
                in_specs=[full, full, full, pl.BlockSpec((1, 6 * half, half), lambda t, on: (t * on[0], 0, 0))],
                out_specs=full,
                scratch_shapes=[pltpu.VMEM((PIX, 6 * half), BF), pltpu.VMEM((3, PIX, half), F32)]),
            compiler_params=_limit(52), name="conv")(turn_on(j), own, oth, a, w)

    def dgrad(j, dy):
        return pl.pallas_call(
            _dgrad_kernel, out_shape=(act32, act),
            grid_spec=pltpu.PrefetchScalarGridSpec(
                num_scalar_prefetch=1, grid=(3,),
                in_specs=[full, pl.BlockSpec((1, 3 * half, 2 * half), lambda t, on: (t * on[0], 0, 0))],
                out_specs=(full, full),
                scratch_shapes=[pltpu.VMEM((PIX, 3 * half), BF), pltpu.VMEM((3, PIX, 2 * half), F32)]),
            compiler_params=_limit(52), name="dgrad")(turn_on(j), dy, w_turned)

    def added(p, q):
        return (p.astype(F32) + q.astype(F32)).astype(BF)

    first = place(first)
    last = place(last)
    first, last, gain, bias, w = lax.optimization_barrier((first, last, gain, bias, w))
    a = jnp.where(segment == 0, first, jnp.zeros_like(first))
    inputs = [a]
    skips = {}
    for j in range(7):
        own = normed(a)
        oth = swap(own)
        y = conv(j, own, oth, a)
        if j == 1:
            late, y = lax.optimization_barrier((w, y))
            late = jnp.transpose(late.reshape(3, 3, 2 * half, half), (0, 1, 3, 2))
        a = move(y, j, j + 1)
        if j == 1:
            late, a = lax.optimization_barrier((late, a))
        if j < 3:
            skips[j] = move(y, j, 7 - j)
        if j >= 4:
            a = added(a, skips[6 - j])
        inputs.append(a)
    mine = inputs[0]
    for a in inputs[1:]:
        mine = mine + a

    hidden, xhat, slope, rstd = prep(mine)
    w_turned = late.reshape(3, 3 * half, 2 * half)

    dy = jnp.where(segment == 7, last, jnp.zeros_like(last))
    grads = []
    gain_sum = bias_sum = 0.0
    skip_grads = {}
    for j in reversed(range(8)):
        if j == 3:
            own_all, oth_all, dy = lax.optimization_barrier((own_all, oth_all, dy))
        if j == 0:
            mine = grads[0]
            for g in grads[1:]:
                mine = mine + g
            mine = mine + dy
            dz = [lax.dynamic_slice_in_dim(mine, (z + by) % 4 * 128, 128, 1) for by in range(4)]
            dz = jnp.stack(dz[:1] + [turn_z(dz[by], by) for by in (1, 2, 3)])
            dz, dy = lax.optimization_barrier((dz, dy))
            turned = [turn(dz, -1), turn(dz, 2), turn(dz, 1)]
            dall = jnp.concatenate([dz] + turned, axis=0)
        grads.append(dy)
        own, oth = dgrad(j, dy)
        oth = swap(oth)
        da, dg, db = pl.pallas_call(
            lambda *r: _gn_bwd_kernel(width, *r), out_shape=(act, line, line),
            compiler_params=_limit(10), name="gn_bwd",
        )(dy, own, oth, xhat, slope, rstd, gain)
        gain_sum = gain_sum + dg
        bias_sum = bias_sum + db
        if j > 0:
            dy = move(da, j, j - 1)
        if j > 4:
            skip_grads[7 - j] = move(da, j, 7 - j)
        if 0 < j < 4:
            dy = added(dy, skip_grads[j - 1])
        if j == 4:
            hidden, dg = lax.optimization_barrier((hidden, dg))
            hz = jnp.stack([hidden] + [turn_z(hidden, by) for by in (1, 2, 3)])
            own_all = jnp.concatenate([hz, turn(hz, -1), turn(hz, 2), turn(hz, 1)], axis=0)
            oth_all = swap(own_all)

    flip = jnp.stack([core, 1 - core]).astype(jnp.int32)
    hspec = pl.BlockSpec((16 * PIX, 128), lambda i, c: (0, i))
    grad_weight = pl.pallas_call(
        _dw_kernel,
        out_shape=jax.ShapeDtypeStruct((9, 2 * half, 128), F32),
        grid_spec=pltpu.PrefetchScalarGridSpec(
            num_scalar_prefetch=1, grid=(4,),
            in_specs=[hspec, hspec, pl.BlockSpec((16, PIX, 128), lambda i, c: (0, 0, 0))],
            out_specs=pl.BlockSpec((9, 256, 128), lambda i, c: (0, i, 0)),
            scratch_shapes=[pltpu.VMEM((3, PIX + 2 * SIDE, 128), BF), pltpu.VMEM((16 * PIX, 9 * 128), BF)]),
        compiler_params=_limit(58), name="dw")(flip, own_all.reshape(16 * PIX, half), oth_all.reshape(16 * PIX, half), dall)

    small = jnp.transpose(jnp.concatenate([gain_sum, bias_sum], axis=0).reshape(2, 4, 128), (1, 0, 2))
    total = lax.dynamic_index_in_dim(small, z, 0, keepdims=False)
    for by in (1, 2, 3):
        piece = lax.dynamic_index_in_dim(small, (z + by) % 4, 0, keepdims=False)
        total = total + turn_z(piece, by)
    total, grad_weight = lax.optimization_barrier((total, grad_weight))
    small = total + turn(total, 1) + turn(total, 2) + turn(total, -1)
    return (grad_weight[None], small[0:1], small[1:2])


def solution(mesh):
    in_specs = (
        P(None, "dp", None, "chan"),
        P(None, "dp", None, "chan"),
        P("segment", None, None, "chan"),
        P("segment", "chan"),
        P("segment", "chan"),
    )
    out_specs = (P("segment", None, None, "chan"), P("segment", "chan"), P("segment", "chan"))

    return jax.shard_map(local, mesh=mesh, in_specs=in_specs, out_specs=out_specs, check_vma=False)
```

```python
import jax
import jax.numpy as jnp
from jax import lax
from jax.experimental import pallas as pl
from jax.experimental.pallas import tpu as pltpu
from jax.sharding import PartitionSpec as P


GROUPS = 32
SIDE = 16
EPSILON = 1e-05
PIX = SIDE * SIDE
BF = jnp.bfloat16
F32 = jnp.float32


def _groups(width):
    r = lax.broadcasted_iota(jnp.int32, (128, 128), 0) // width
    c = lax.broadcasted_iota(jnp.int32, (128, 128), 1) // width
    return jnp.where(r == c, 1.0, 0.0).astype(BF)


def _group_sum(v, ones):
    n = v.shape[1] // 128
    rows = jnp.concatenate([v[:, i * 128:(i + 1) * 128] for i in range(n)], axis=0)
    hi = rows.astype(BF)
    rest = rows - hi.astype(F32)
    mid = rest.astype(BF)
    low = (rest - mid.astype(F32)).astype(BF)
    out = (jnp.dot(hi, ones, preferred_element_type=F32)
           + jnp.dot(mid, ones, preferred_element_type=F32)
           + jnp.dot(low, ones, preferred_element_type=F32))
    return jnp.concatenate([out[i:i + 1] for i in range(n)], axis=1)


def _normalized(a, count, width):
    ones = _groups(width)
    v = a.astype(F32)
    mean = _group_sum(jnp.sum(v, axis=0, keepdims=True), ones) * (1.0 / count)
    cen = v - mean
    var = _group_sum(jnp.sum(cen * cen, axis=0, keepdims=True), ones) * (1.0 / count)
    rstd = lax.rsqrt(var + EPSILON)
    return cen * rstd, rstd


def _gn_kernel(width, a_ref, gain_ref, bias_ref, h_ref):
    xhat, _ = _normalized(a_ref[...], PIX * width, width)
    n = xhat * gain_ref[...] + bias_ref[...]
    h_ref[...] = (n * jax.nn.sigmoid(n)).astype(BF)


def _prep_kernel(width, a_ref, gain_ref, bias_ref, h_ref, xhat_ref, slope_ref, rstd_ref):
    xhat, rstd = _normalized(a_ref[...], PIX * width, width)
    n = xhat * gain_ref[...] + bias_ref[...]
    s = jax.nn.sigmoid(n)
    h_ref[...] = (n * s).astype(BF)
    xhat_ref[...] = xhat
    slope_ref[...] = s * (1.0 + n * (1.0 - s))
    rstd_ref[...] = rstd


def _gn_bwd_kernel(width, dy_ref, own_ref, oth_ref, xhat_ref, slope_ref, rstd_ref, gain_ref,
                   da_ref, dg_ref, db_ref):
    ones = _groups(width)
    count = PIX * width
    dn = (own_ref[...] + oth_ref[...].astype(F32)) * slope_ref[...]
    xhat = xhat_ref[...]
    gain = gain_ref[...]
    db = jnp.sum(dn, axis=0, keepdims=True)
    dg = jnp.sum(dn * xhat, axis=0, keepdims=True)
    m1 = _group_sum(db * gain, ones) * (1.0 / count)
    m2 = _group_sum(dg * gain, ones) * (1.0 / count)
    da = dy_ref[...].astype(F32) + rstd_ref[...] * (dn * gain - m1 - xhat * m2)
    da_ref[...] = da.astype(BF)
    dg_ref[...] = dg
    db_ref[...] = db


def _pad_into(ref, value):
    zero = jnp.zeros((SIDE, ref.shape[1]), ref.dtype)
    ref[0:SIDE, :] = zero
    ref[SIDE:SIDE + PIX, :] = value
    ref[SIDE + PIX:, :] = zero


def _join_shifts(left, mid, right):
    x = lax.broadcasted_iota(jnp.int32, mid.shape, 0) % SIDE
    out = mid + jnp.where(x > 0, pltpu.roll(left, 1, 0), 0.0)
    return out + jnp.where(x < SIDE - 1, pltpu.roll(right, PIX - 1, 0), 0.0)


def _cat_into(ref, col, value, turn):
    wide = value.shape[1]
    zero = jnp.zeros((SIDE, wide), value.dtype)
    for ky in range(3):
        lo = ky * (ref.shape[1] // 3) + col
        by = (ky - 1) * turn
        if by == 0:
            ref[:, lo:lo + wide] = value
        elif by < 0:
            ref[0:SIDE, lo:lo + wide] = zero
            ref[SIDE:, lo:lo + wide] = value[:PIX - SIDE]
        else:
            ref[0:PIX - SIDE, lo:lo + wide] = value[SIDE:]
            ref[PIX - SIDE:, lo:lo + wide] = zero


def _conv_kernel(on_ref, own_ref, oth_ref, a_ref, w_ref, y_ref, cat_ref, acc_ref):
    kx = pl.program_id(0)

    @pl.when(on_ref[0] > 0)
    def _():
        _conv_step(kx, own_ref, oth_ref, a_ref, w_ref, y_ref, cat_ref, acc_ref)

    @pl.when((on_ref[0] == 0) & (kx == 0))
    def _():
        y_ref[...] = jnp.zeros_like(y_ref)


def _conv_step(kx, own_ref, oth_ref, a_ref, w_ref, y_ref, cat_ref, acc_ref):

    @pl.when(kx == 0)
    def _():
        _cat_into(cat_ref, 0, own_ref[...], 1)
        _cat_into(cat_ref, own_ref.shape[1], oth_ref[...], 1)

    acc_ref[kx] = jnp.dot(cat_ref[...], w_ref[0], preferred_element_type=F32)

    @pl.when(kx == 2)
    def _():
        z = _join_shifts(acc_ref[0], acc_ref[1], acc_ref[2])
        y_ref[...] = (a_ref[...].astype(F32) + z).astype(BF)


def _dgrad_kernel(on_ref, dy_ref, w_ref, own_ref, oth_ref, cat_ref, acc_ref):
    kx = pl.program_id(0)

    @pl.when(on_ref[0] > 0)
    def _():
        _dgrad_step(kx, dy_ref, w_ref, own_ref, oth_ref, cat_ref, acc_ref)

    @pl.when((on_ref[0] == 0) & (kx == 0))
    def _():
        own_ref[...] = jnp.zeros_like(own_ref)
        oth_ref[...] = jnp.zeros_like(oth_ref)


def _dgrad_step(kx, dy_ref, w_ref, own_ref, oth_ref, cat_ref, acc_ref):

    @pl.when(kx == 0)
    def _():
        _cat_into(cat_ref, 0, dy_ref[...], -1)

    acc_ref[kx] = jnp.dot(cat_ref[...], w_ref[0], preferred_element_type=F32)

    @pl.when(kx == 2)
    def _():
        half = dy_ref.shape[1]
        p = _join_shifts(acc_ref[2], acc_ref[1], acc_ref[0])
        own_ref[...] = p[:, :half]
        oth_ref[...] = p[:, half:].astype(BF)


def _dw_kernel(idx_ref, *refs):
    own, oth, dys = refs[0:5], refs[5:10], refs[10:14]
    out_ref, pad_ref, rhs_ref = refs[14:]

    @pl.when(pl.program_id(0) == 0)
    def _():
        x = lax.broadcasted_iota(jnp.int32, (PIX, 128), 0) % SIDE
        for g in range(4):
            def build(i, carry):
                v = dys[g][i].astype(F32)
                moved = (jnp.where(x < SIDE - 1, pltpu.roll(v, PIX - 1, 0), 0.0), v,
                         jnp.where(x > 0, pltpu.roll(v, 1, 0), 0.0))
                for kx in range(3):
                    _pad_into(pad_ref.at[kx], moved[kx].astype(BF))
                for t in range(9):
                    start = (2 - t // 3) * SIDE
                    at = pl.multiple_of((g * 4 + i) * PIX, PIX)
                    rhs_ref[pl.ds(at, PIX), t * 128:(t + 1) * 128] = pad_ref[t % 3, start:start + PIX, :]
                return carry

            lax.fori_loop(0, 4, build, 0)

    h = jnp.concatenate([jnp.concatenate([p[...], q[...]], axis=1) for p, q in zip(own, oth)], axis=0)
    for lo, taps in ((0, 2), (2, 2), (4, 2), (6, 2), (8, 1)):
        part = lax.dot_general(h, rhs_ref[:, lo * 128:(lo + taps) * 128], (((0,), (0,)), ((), ())),
                               preferred_element_type=F32)
        for i in range(taps):
            for side in range(2):
                at = pl.multiple_of(idx_ref[side] * 128, 128)
                out_ref[lo + i, pl.ds(at, 128), :] = part[side * 128:(side + 1) * 128, i * 128:(i + 1) * 128]


def _assemble_kernel(idx_ref, near, up, down, far0, far1, *rest):
    out_ref = rest[-1]
    for side in range(2):
        at = idx_ref[4 + side]
        for kx in range(3):
            out_ref[kx, 0, at, idx_ref[0]] = near[side, kx]
            out_ref[kx, 0, at, idx_ref[1]] = up[side, kx]
            out_ref[kx, 0, at, idx_ref[2]] = (far0, far1)[side][kx]
            out_ref[kx, 0, at, idx_ref[3]] = down[side, kx]


def _place_kernel(idx_ref, *refs):
    for by in range(4):
        refs[4][:, pl.ds(pl.multiple_of(idx_ref[by] * 128, 128), 128)] = refs[by][...]


def _limit(mib):
    return pltpu.CompilerParams(vmem_limit_bytes=mib << 20)


def local(x_input, d_output, weights, gains, biases):
    row = lax.axis_index("dp")
    segment = lax.axis_index("segment")
    chan = lax.axis_index("chan")
    z = chan // 2
    core = chan % 2
    width = weights.shape[2] // GROUPS
    half = 4 * 128
    axes = ("dp", "segment", "chan")

    def lin(d, s, k):
        return (d * 8 + s) * 8 + k

    def move(value, source, target):
        flip = (source < 4) != (target < 4)
        pairs = [(lin(d, source, k), lin(d, target, (6 - k + 2 * (k % 2)) if flip else k))
                 for d in range(4) for k in range(8)]
        return lax.ppermute(value, axes, pairs)

    def swap(value):
        return lax.ppermute(value, "chan", [(k, k ^ 1) for k in range(8)])

    def turn(value, by):
        return lax.ppermute(value, "dp", [(i, (i + by) % 4) for i in range(4)])

    def turn_z(value, by):
        return lax.ppermute(value, "chan", [(k, (k + 2 * by) % 8) for k in range(8)])

    sources = ((z - jnp.arange(4)) % 4).astype(jnp.int32)

    def send(pick):
        return [pick(z)] + [turn_z(pick((z + by) % 4), by) for by in (1, 2, 3)]

    def place(parts):
        shape = jax.ShapeDtypeStruct((parts[0].shape[0], half), parts[0].dtype)
        return pl.pallas_call(
            _place_kernel, out_shape=shape,
            grid_spec=pltpu.PrefetchScalarGridSpec(
                num_scalar_prefetch=1, grid=(1,),
                in_specs=[pl.BlockSpec(parts[0].shape, lambda t, i: (0, 0))] * 4,
                out_specs=pl.BlockSpec(shape.shape, lambda t, i: (0, 0))),
            compiler_params=_limit(6), name="place")(sources, *parts)

    rows = jnp.concatenate([gains, biases], axis=0)
    rows = send(lambda t: rows)
    first = send(lambda t: lax.dynamic_index_in_dim(x_input[:, 0], t, 0, keepdims=False))

    quarter = lax.dynamic_slice_in_dim(weights[0], row * 256, 256, 1)
    quarter = jnp.transpose(quarter.reshape(9, 2, 128, 128), (1, 0, 2, 3))
    rows, first, quarter = lax.optimization_barrier((rows, first, quarter))
    rows = place(rows)
    first = place(first)
    sides = [(row + jnp.arange(4)) % 4, (core + jnp.arange(2)) % 2]
    token = None
    pieces = {}

    def assemble(by, w=None):
        places = jnp.concatenate(sides + [(z - by)[None] % 4]).astype(jnp.int32)
        return pl.pallas_call(
            _assemble_kernel,
            out_shape=jax.ShapeDtypeStruct((3, 3, 2, 4, 128, half), BF),
            grid_spec=pltpu.PrefetchScalarGridSpec(
                num_scalar_prefetch=1, grid=(3,),
                in_specs=[pl.BlockSpec((2, 3, 128, 128), lambda t, i: (0, t, 0, 0))] * 3
                + [pl.BlockSpec((3, 128, 128), lambda t, i: (t, 0, 0))] * 2
                + ([] if w is None else [pl.BlockSpec(memory_space=pl.ANY)]),
                out_specs=pl.BlockSpec((3, 1, 2, 4, 128, 128), lambda t, i: (0, t, 0, 0, 0, i[6]))),
            input_output_aliases={} if w is None else {6: 0},
            compiler_params=_limit(52), name="assemble",
        )(places, *pieces[by], *([] if w is None else [w]))

    for by in (0, 1, 3, 2):
        piece = quarter
        if by > 1:
            piece, token = lax.optimization_barrier((piece, token))
        if by > 0:
            piece = turn_z(piece, by)
        if by == 1:
            piece, rows, first = lax.optimization_barrier((piece, rows, first))
        token = piece
        below = turn(piece, 1)
        above = turn(piece, -1)
        if by == 2:
            w = assemble(1, assemble(0))
            below, above, w = lax.optimization_barrier((below, above, w))
        far = [turn(below[0], 1), turn(above[1], -1)]
        pieces[by] = [piece, above, below] + far
    w = assemble(2, assemble(3, w))
    w = w.reshape(3, 6 * half, half)

    gain = rows[0:1]
    bias = rows[1:2]

    act = jax.ShapeDtypeStruct((PIX, half), BF)
    act32 = jax.ShapeDtypeStruct((PIX, half), F32)
    line = jax.ShapeDtypeStruct((1, half), F32)

    def normed(a):
        return pl.pallas_call(lambda *r: _gn_kernel(width, *r), out_shape=act, compiler_params=_limit(6), name="gn")(a, gain, bias)

    def prep(a):
        return pl.pallas_call(lambda *r: _prep_kernel(width, *r), out_shape=(act, act32, act32, line),
                              compiler_params=_limit(10), name="prep")(a, gain, bias)

    full = pl.BlockSpec((PIX, half), lambda t, on: (0, 0))

    def turn_on(j):
        return jnp.where(segment == j, 1, 0).astype(jnp.int32).reshape(1)

    def conv(j, own, oth, a):
        return pl.pallas_call(
            _conv_kernel, out_shape=act,
            grid_spec=pltpu.PrefetchScalarGridSpec(
                num_scalar_prefetch=1, grid=(3,),
                in_specs=[full, full, full, pl.BlockSpec((1, 6 * half, half), lambda t, on: (t * on[0], 0, 0))],
                out_specs=full,
                scratch_shapes=[pltpu.VMEM((PIX, 6 * half), BF), pltpu.VMEM((3, PIX, half), F32)]),
            compiler_params=_limit(52), name="conv")(turn_on(j), own, oth, a, w)

    def dgrad(j, dy):
        return pl.pallas_call(
            _dgrad_kernel, out_shape=(act32, act),
            grid_spec=pltpu.PrefetchScalarGridSpec(
                num_scalar_prefetch=1, grid=(3,),
                in_specs=[full, pl.BlockSpec((1, 3 * half, 2 * half), lambda t, on: (t * on[0], 0, 0))],
                out_specs=(full, full),
                scratch_shapes=[pltpu.VMEM((PIX, 3 * half), BF), pltpu.VMEM((3, PIX, 2 * half), F32)]),
            compiler_params=_limit(52), name="dgrad")(turn_on(j), dy, w_turned)

    def added(p, q):
        return (p.astype(F32) + q.astype(F32)).astype(BF)

    first, gain, bias, w = lax.optimization_barrier((first, gain, bias, w))
    a = jnp.where(segment == 0, first, jnp.zeros_like(first))
    inputs = [a]
    skips = {}
    for j in range(7):
        own = normed(a)
        oth = swap(own)
        y = conv(j, own, oth, a)
        if j == 1:
            late, end, y = lax.optimization_barrier((w, d_output[:, 0], y))
            last = place(send(lambda t: lax.dynamic_index_in_dim(end, 3 - t, 0, keepdims=False)))
            late = jnp.transpose(late.reshape(3, 3, 2 * half, half), (0, 1, 3, 2))
        a = move(y, j, j + 1)
        if j == 1:
            late, last, a = lax.optimization_barrier((late, last, a))
        if j < 3:
            skips[j] = move(y, j, 7 - j)
        if j >= 4:
            a = added(a, skips[6 - j])
        inputs.append(a)
    mine = inputs[0]
    for a in inputs[1:]:
        mine = mine + a

    hidden, xhat, slope, rstd = prep(mine)
    w_turned = late.reshape(3, 3 * half, 2 * half)

    dy = jnp.where(segment == 7, last, jnp.zeros_like(last))
    grads = []
    gain_sum = bias_sum = 0.0
    skip_grads = {}
    for j in reversed(range(8)):
        if j == 0:
            mine = grads[0]
            for g in grads[1:]:
                mine = mine + g
            mine = mine + dy
            dz = [lax.dynamic_slice_in_dim(mine, (z + by) % 4 * 128, 128, 1) for by in range(4)]
            dz = jnp.stack(dz[:1] + [turn_z(dz[by], by) for by in (1, 2, 3)])
            dz, dy = lax.optimization_barrier((dz, dy))
            turned = [turn(dz, -1), turn(dz, 2), turn(dz, 1)]
            dall = [dz] + turned
        grads.append(dy)
        own, oth = dgrad(j, dy)
        oth = swap(oth)
        da, dg, db = pl.pallas_call(
            lambda *r: _gn_bwd_kernel(width, *r), out_shape=(act, line, line),
            compiler_params=_limit(10), name="gn_bwd",
        )(dy, own, oth, xhat, slope, rstd, gain)
        gain_sum = gain_sum + dg
        bias_sum = bias_sum + db
        if j > 0:
            dy = move(da, j, j - 1)
        if j > 4:
            skip_grads[7 - j] = move(da, j, 7 - j)
        if 0 < j < 4:
            dy = added(dy, skip_grads[j - 1])
        if j == 4:
            hidden, dg = lax.optimization_barrier((hidden, dg))
            hz = jnp.stack([hidden] + [turn_z(hidden, by) for by in (1, 2, 3)])
            h_up = turn(hz, -1)
            h_down = turn(hz, 1)
            h_far = [turn(h_down[:2], 1), turn(h_up[2:], -1)]
            own_all = [hz, h_up] + h_far + [h_down]
            oth_all = [swap(h) for h in own_all]

    flip = jnp.stack([core, 1 - core]).astype(jnp.int32)
    parts = [h.reshape(-1, half) for h in own_all + oth_all]
    grad_weight = pl.pallas_call(
        _dw_kernel,
        out_shape=jax.ShapeDtypeStruct((9, 2 * half, 128), F32),
        grid_spec=pltpu.PrefetchScalarGridSpec(
            num_scalar_prefetch=1, grid=(4,),
            in_specs=[pl.BlockSpec((p.shape[0], 128), lambda i, c: (0, i)) for p in parts] + [pl.BlockSpec((4, PIX, 128), lambda i, c: (0, 0, 0))] * 4,
            out_specs=pl.BlockSpec((9, 256, 128), lambda i, c: (0, i, 0)),
            scratch_shapes=[pltpu.VMEM((3, PIX + 2 * SIDE, 128), BF), pltpu.VMEM((16 * PIX, 9 * 128), BF)]),
        compiler_params=_limit(52), name="dw",
    )(flip, *parts, *dall)

    small = jnp.transpose(jnp.concatenate([gain_sum, bias_sum], axis=0).reshape(2, 4, 128), (1, 0, 2))
    total = lax.dynamic_index_in_dim(small, z, 0, keepdims=False)
    for by in (1, 2, 3):
        piece = lax.dynamic_index_in_dim(small, (z + by) % 4, 0, keepdims=False)
        total = total + turn_z(piece, by)
    total, grad_weight = lax.optimization_barrier((total, grad_weight))
    for bit in (1, 2):
        total = total + lax.ppermute(total, "dp", [(i, i ^ bit) for i in range(4)])
    small = total
    return (grad_weight[None], small[0:1], small[1:2])


def solution(mesh):
    in_specs = (
        P(None, "dp", None, "chan"),
        P(None, "dp", None, "chan"),
        P("segment", None, None, "chan"),
        P("segment", "chan"),
        P("segment", "chan"),
    )
    out_specs = (P("segment", None, None, "chan"), P("segment", "chan"), P("segment", "chan"))

    return jax.shard_map(local, mesh=mesh, in_specs=in_specs, out_specs=out_specs, check_vma=False)
```

```python
import jax
import jax.numpy as jnp
from jax import lax
from jax.experimental import pallas as pl
from jax.experimental.pallas import tpu as pltpu
from jax.sharding import PartitionSpec as P


GROUPS = 32
SIDE = 16
EPSILON = 1e-05
PIX = SIDE * SIDE
BF = jnp.bfloat16
F32 = jnp.float32


def _groups(width):
    r = lax.broadcasted_iota(jnp.int32, (128, 128), 0) // width
    c = lax.broadcasted_iota(jnp.int32, (128, 128), 1) // width
    return jnp.where(r == c, 1.0, 0.0).astype(BF)


def _group_sum(v, ones):
    n = v.shape[1] // 128
    rows = jnp.concatenate([v[:, i * 128:(i + 1) * 128] for i in range(n)], axis=0)
    hi = rows.astype(BF)
    rest = rows - hi.astype(F32)
    mid = rest.astype(BF)
    low = (rest - mid.astype(F32)).astype(BF)
    out = (jnp.dot(hi, ones, preferred_element_type=F32)
           + jnp.dot(mid, ones, preferred_element_type=F32)
           + jnp.dot(low, ones, preferred_element_type=F32))
    return jnp.concatenate([out[i:i + 1] for i in range(n)], axis=1)


def _normalized(a, count, width):
    ones = _groups(width)
    v = a.astype(F32)
    mean = _group_sum(jnp.sum(v, axis=0, keepdims=True), ones) * (1.0 / count)
    cen = v - mean
    var = _group_sum(jnp.sum(cen * cen, axis=0, keepdims=True), ones) * (1.0 / count)
    rstd = lax.rsqrt(var + EPSILON)
    return cen * rstd, rstd


def _gn_kernel(width, a_ref, gain_ref, bias_ref, h_ref):
    xhat, _ = _normalized(a_ref[...], PIX * width, width)
    n = xhat * gain_ref[...] + bias_ref[...]
    h_ref[...] = (n * jax.nn.sigmoid(n)).astype(BF)


def _prep_kernel(width, a_ref, gain_ref, bias_ref, h_ref, xhat_ref, slope_ref, rstd_ref):
    xhat, rstd = _normalized(a_ref[...], PIX * width, width)
    n = xhat * gain_ref[...] + bias_ref[...]
    s = jax.nn.sigmoid(n)
    h_ref[...] = (n * s).astype(BF)
    xhat_ref[...] = xhat
    slope_ref[...] = s * (1.0 + n * (1.0 - s))
    rstd_ref[...] = rstd


def _gn_bwd_kernel(width, dy_ref, own_ref, oth_ref, xhat_ref, slope_ref, rstd_ref, gain_ref,
                   da_ref, dg_ref, db_ref):
    ones = _groups(width)
    count = PIX * width
    dn = (own_ref[...] + oth_ref[...].astype(F32)) * slope_ref[...]
    xhat = xhat_ref[...]
    gain = gain_ref[...]
    db = jnp.sum(dn, axis=0, keepdims=True)
    dg = jnp.sum(dn * xhat, axis=0, keepdims=True)
    m1 = _group_sum(db * gain, ones) * (1.0 / count)
    m2 = _group_sum(dg * gain, ones) * (1.0 / count)
    da = dy_ref[...].astype(F32) + rstd_ref[...] * (dn * gain - m1 - xhat * m2)
    da_ref[...] = da.astype(BF)
    dg_ref[...] = dg
    db_ref[...] = db


def _pad_into(ref, value):
    zero = jnp.zeros((SIDE, ref.shape[1]), ref.dtype)
    ref[0:SIDE, :] = zero
    ref[SIDE:SIDE + PIX, :] = value
    ref[SIDE + PIX:, :] = zero


def _join_shifts(left, mid, right):
    x = lax.broadcasted_iota(jnp.int32, mid.shape, 0) % SIDE
    out = mid + jnp.where(x > 0, pltpu.roll(left, 1, 0), 0.0)
    return out + jnp.where(x < SIDE - 1, pltpu.roll(right, PIX - 1, 0), 0.0)


def _cat_into(ref, col, value, turn):
    wide = value.shape[1]
    zero = jnp.zeros((SIDE, wide), value.dtype)
    for ky in range(3):
        lo = ky * (ref.shape[1] // 3) + col
        by = (ky - 1) * turn
        if by == 0:
            ref[:, lo:lo + wide] = value
        elif by < 0:
            ref[0:SIDE, lo:lo + wide] = zero
            ref[SIDE:, lo:lo + wide] = value[:PIX - SIDE]
        else:
            ref[0:PIX - SIDE, lo:lo + wide] = value[SIDE:]
            ref[PIX - SIDE:, lo:lo + wide] = zero


def _conv_kernel(on_ref, own_ref, oth_ref, a_ref, w_ref, y_ref, cat_ref, acc_ref):
    kx = pl.program_id(0)

    @pl.when(on_ref[0] > 0)
    def _():
        _conv_step(kx, own_ref, oth_ref, a_ref, w_ref, y_ref, cat_ref, acc_ref)

    @pl.when((on_ref[0] == 0) & (kx == 0))
    def _():
        y_ref[...] = jnp.zeros_like(y_ref)


def _conv_step(kx, own_ref, oth_ref, a_ref, w_ref, y_ref, cat_ref, acc_ref):

    @pl.when(kx == 0)
    def _():
        _cat_into(cat_ref, 0, own_ref[...], 1)
        _cat_into(cat_ref, own_ref.shape[1], oth_ref[...], 1)

    acc_ref[kx] = jnp.dot(cat_ref[...], w_ref[0], preferred_element_type=F32)

    @pl.when(kx == 2)
    def _():
        z = _join_shifts(acc_ref[0], acc_ref[1], acc_ref[2])
        y_ref[...] = (a_ref[...].astype(F32) + z).astype(BF)


def _dgrad_kernel(on_ref, dy_ref, w_ref, own_ref, oth_ref, cat_ref, acc_ref):
    kx = pl.program_id(0)

    @pl.when(on_ref[0] > 0)
    def _():
        _dgrad_step(kx, dy_ref, w_ref, own_ref, oth_ref, cat_ref, acc_ref)

    @pl.when((on_ref[0] == 0) & (kx == 0))
    def _():
        own_ref[...] = jnp.zeros_like(own_ref)
        oth_ref[...] = jnp.zeros_like(oth_ref)


def _dgrad_step(kx, dy_ref, w_ref, own_ref, oth_ref, cat_ref, acc_ref):

    @pl.when(kx == 0)
    def _():
        _cat_into(cat_ref, 0, dy_ref[...], -1)

    acc_ref[kx] = jnp.dot(cat_ref[...], w_ref[0], preferred_element_type=F32)

    @pl.when(kx == 2)
    def _():
        half = dy_ref.shape[1]
        p = _join_shifts(acc_ref[2], acc_ref[1], acc_ref[0])
        own_ref[...] = p[:, :half]
        oth_ref[...] = p[:, half:].astype(BF)


def _dw_kernel(idx_ref, *refs):
    own, oth, dys = refs[0:5], refs[5:10], refs[10:14]
    out_ref, pad_ref, rhs_ref = refs[14:]

    @pl.when(pl.program_id(0) == 0)
    def _():
        x = lax.broadcasted_iota(jnp.int32, (PIX, 128), 0) % SIDE
        for g in range(4):
            def build(i, carry):
                v = dys[g][i].astype(F32)
                moved = (jnp.where(x < SIDE - 1, pltpu.roll(v, PIX - 1, 0), 0.0), v,
                         jnp.where(x > 0, pltpu.roll(v, 1, 0), 0.0))
                for kx in range(3):
                    _pad_into(pad_ref.at[kx], moved[kx].astype(BF))
                for t in range(9):
                    start = (2 - t // 3) * SIDE
                    at = pl.multiple_of((g * 4 + i) * PIX, PIX)
                    rhs_ref[pl.ds(at, PIX), t * 128:(t + 1) * 128] = pad_ref[t % 3, start:start + PIX, :]
                return carry

            lax.fori_loop(0, 4, build, 0)

    h = jnp.concatenate([jnp.concatenate([p[...], q[...]], axis=1) for p, q in zip(own, oth)], axis=0)
    for lo, taps in ((0, 2), (2, 2), (4, 2), (6, 2), (8, 1)):
        part = lax.dot_general(h, rhs_ref[:, lo * 128:(lo + taps) * 128], (((0,), (0,)), ((), ())),
                               preferred_element_type=F32)
        for i in range(taps):
            for side in range(2):
                at = pl.multiple_of(idx_ref[side] * 128, 128)
                out_ref[lo + i, pl.ds(at, 128), :] = part[side * 128:(side + 1) * 128, i * 128:(i + 1) * 128]


def _assemble_kernel(idx_ref, near, up, down, far0, far1, *rest):
    out_ref = rest[-1]
    for side in range(2):
        at = idx_ref[4 + side]
        for kx in range(3):
            out_ref[kx, 0, at, idx_ref[0]] = near[side, kx]
            out_ref[kx, 0, at, idx_ref[1]] = up[side, kx]
            out_ref[kx, 0, at, idx_ref[2]] = (far0, far1)[side][kx]
            out_ref[kx, 0, at, idx_ref[3]] = down[side, kx]


def _place_kernel(idx_ref, *refs):
    for by in range(4):
        refs[4][:, pl.ds(pl.multiple_of(idx_ref[by] * 128, 128), 128)] = refs[by][...]


def _limit(mib):
    return pltpu.CompilerParams(vmem_limit_bytes=mib << 20)


def local(x_input, d_output, weights, gains, biases):
    row = lax.axis_index("dp")
    segment = lax.axis_index("segment")
    chan = lax.axis_index("chan")
    z = chan // 2
    core = chan % 2
    width = weights.shape[2] // GROUPS
    half = 4 * 128
    axes = ("dp", "segment", "chan")

    def lin(d, s, k):
        return (d * 8 + s) * 8 + k

    def move(value, source, target):
        flip = (source < 4) != (target < 4)
        pairs = [(lin(d, source, k), lin(d, target, (6 - k + 2 * (k % 2)) if flip else k))
                 for d in range(4) for k in range(8)]
        return lax.ppermute(value, axes, pairs)

    def swap(value):
        return lax.ppermute(value, "chan", [(k, k ^ 1) for k in range(8)])

    def turn(value, by):
        return lax.ppermute(value, "dp", [(i, (i + by) % 4) for i in range(4)])

    def turn_z(value, by):
        return lax.ppermute(value, "chan", [(k, (k + 2 * by) % 8) for k in range(8)])

    sources = ((z - jnp.arange(4)) % 4).astype(jnp.int32)

    def send(pick):
        return [pick(z)] + [turn_z(pick((z + by) % 4), by) for by in (1, 2, 3)]

    def place(parts):
        shape = jax.ShapeDtypeStruct((parts[0].shape[0], half), parts[0].dtype)
        return pl.pallas_call(
            _place_kernel, out_shape=shape,
            grid_spec=pltpu.PrefetchScalarGridSpec(
                num_scalar_prefetch=1, grid=(1,),
                in_specs=[pl.BlockSpec(parts[0].shape, lambda t, i: (0, 0))] * 4,
                out_specs=pl.BlockSpec(shape.shape, lambda t, i: (0, 0))),
            compiler_params=_limit(6), name="place")(sources, *parts)

    rows = jnp.concatenate([gains, biases], axis=0)
    rows = send(lambda t: rows)
    first = send(lambda t: lax.dynamic_index_in_dim(x_input[:, 0], t, 0, keepdims=False))

    quarter = lax.dynamic_slice_in_dim(weights[0], row * 256, 256, 1)
    quarter = jnp.transpose(quarter.reshape(9, 2, 128, 128), (1, 0, 2, 3))
    rows, first, quarter = lax.optimization_barrier((rows, first, quarter))
    rows = place(rows)
    first = place(first)
    sides = [(row + jnp.arange(4)) % 4, (core + jnp.arange(2)) % 2]
    token = None
    pieces = {}

    def assemble(by, w=None):
        places = jnp.concatenate(sides + [(z - by)[None] % 4]).astype(jnp.int32)
        return pl.pallas_call(
            _assemble_kernel,
            out_shape=jax.ShapeDtypeStruct((3, 3, 2, 4, 128, half), BF),
            grid_spec=pltpu.PrefetchScalarGridSpec(
                num_scalar_prefetch=1, grid=(3,),
                in_specs=[pl.BlockSpec((2, 3, 128, 128), lambda t, i: (0, t, 0, 0))] * 3
                + [pl.BlockSpec((3, 128, 128), lambda t, i: (t, 0, 0))] * 2
                + ([] if w is None else [pl.BlockSpec(memory_space=pl.ANY)]),
                out_specs=pl.BlockSpec((3, 1, 2, 4, 128, 128), lambda t, i: (0, t, 0, 0, 0, i[6]))),
            input_output_aliases={} if w is None else {6: 0},
            compiler_params=_limit(52), name="assemble",
        )(places, *pieces[by], *([] if w is None else [w]))

    for by in (0, 1, 3, 2):
        piece = quarter
        if by > 1:
            piece, token = lax.optimization_barrier((piece, token))
        if by > 0:
            piece = turn_z(piece, by)
        if by == 1:
            piece, rows, first = lax.optimization_barrier((piece, rows, first))
        token = piece
        below = turn(piece, 1)
        above = turn(piece, -1)
        far = [turn(below[0], 1), turn(above[1], -1)]
        pieces[by] = [piece, above, below] + far
    w = None
    for by in (0, 1, 3, 2):
        w = assemble(by, w)
    w = w.reshape(3, 6 * half, half)

    gain = rows[0:1]
    bias = rows[1:2]

    act = jax.ShapeDtypeStruct((PIX, half), BF)
    act32 = jax.ShapeDtypeStruct((PIX, half), F32)
    line = jax.ShapeDtypeStruct((1, half), F32)

    def normed(a):
        return pl.pallas_call(lambda *r: _gn_kernel(width, *r), out_shape=act, compiler_params=_limit(6), name="gn")(a, gain, bias)

    def prep(a):
        return pl.pallas_call(lambda *r: _prep_kernel(width, *r), out_shape=(act, act32, act32, line),
                              compiler_params=_limit(10), name="prep")(a, gain, bias)

    full = pl.BlockSpec((PIX, half), lambda t, on: (0, 0))

    def turn_on(j):
        return jnp.where(segment == j, 1, 0).astype(jnp.int32).reshape(1)

    def conv(j, own, oth, a):
        return pl.pallas_call(
            _conv_kernel, out_shape=act,
            grid_spec=pltpu.PrefetchScalarGridSpec(
                num_scalar_prefetch=1, grid=(3,),
                in_specs=[full, full, full, pl.BlockSpec((1, 6 * half, half), lambda t, on: (t * on[0], 0, 0))],
                out_specs=full,
                scratch_shapes=[pltpu.VMEM((PIX, 6 * half), BF), pltpu.VMEM((3, PIX, half), F32)]),
            compiler_params=_limit(52), name="conv")(turn_on(j), own, oth, a, w)

    def dgrad(j, dy):
        return pl.pallas_call(
            _dgrad_kernel, out_shape=(act32, act),
            grid_spec=pltpu.PrefetchScalarGridSpec(
                num_scalar_prefetch=1, grid=(3,),
                in_specs=[full, pl.BlockSpec((1, 3 * half, 2 * half), lambda t, on: (t * on[0], 0, 0))],
                out_specs=(full, full),
                scratch_shapes=[pltpu.VMEM((PIX, 3 * half), BF), pltpu.VMEM((3, PIX, 2 * half), F32)]),
            compiler_params=_limit(52), name="dgrad")(turn_on(j), dy, w_turned)

    def added(p, q):
        return (p.astype(F32) + q.astype(F32)).astype(BF)

    first, gain, bias, w = lax.optimization_barrier((first, gain, bias, w))
    a = jnp.where(segment == 0, first, jnp.zeros_like(first))
    inputs = [a]
    skips = {}
    for j in range(7):
        own = normed(a)
        oth = swap(own)
        y = conv(j, own, oth, a)
        if j == 1:
            late, end, y = lax.optimization_barrier((w, d_output[:, 0], y))
            last = place(send(lambda t: lax.dynamic_index_in_dim(end, 3 - t, 0, keepdims=False)))
            late = jnp.transpose(late.reshape(3, 3, 2 * half, half), (0, 1, 3, 2))
        a = move(y, j, j + 1)
        if j == 1:
            late, last, a = lax.optimization_barrier((late, last, a))
        if j < 3:
            skips[j] = move(y, j, 7 - j)
        if j >= 4:
            a = added(a, skips[6 - j])
        inputs.append(a)
    mine = inputs[0]
    for a in inputs[1:]:
        mine = mine + a

    hidden, xhat, slope, rstd = prep(mine)
    w_turned = late.reshape(3, 3 * half, 2 * half)

    dy = jnp.where(segment == 7, last, jnp.zeros_like(last))
    grads = []
    gain_sum = bias_sum = 0.0
    skip_grads = {}
    for j in reversed(range(8)):
        if j == 0:
            mine = grads[0]
            for g in grads[1:]:
                mine = mine + g
            mine = mine + dy
            dz = [lax.dynamic_slice_in_dim(mine, (z + by) % 4 * 128, 128, 1) for by in range(4)]
            dz = jnp.stack(dz[:1] + [turn_z(dz[by], by) for by in (1, 2, 3)])
            dz, dy = lax.optimization_barrier((dz, dy))
            turned = [turn(dz, -1), turn(dz, 2), turn(dz, 1)]
            dall = [dz] + turned
        grads.append(dy)
        own, oth = dgrad(j, dy)
        oth = swap(oth)
        da, dg, db = pl.pallas_call(
            lambda *r: _gn_bwd_kernel(width, *r), out_shape=(act, line, line),
            compiler_params=_limit(10), name="gn_bwd",
        )(dy, own, oth, xhat, slope, rstd, gain)
        gain_sum = gain_sum + dg
        bias_sum = bias_sum + db
        if j > 0:
            dy = move(da, j, j - 1)
        if j > 4:
            skip_grads[7 - j] = move(da, j, 7 - j)
        if 0 < j < 4:
            dy = added(dy, skip_grads[j - 1])
        if j == 4:
            hidden, dg = lax.optimization_barrier((hidden, dg))
            hz = jnp.stack([hidden] + [turn_z(hidden, by) for by in (1, 2, 3)])
            _, dy = lax.optimization_barrier((hz, dy))
            h_up = turn(hz, -1)
            h_down = turn(hz, 1)
            h_far = [turn(h_down[:2], 1), turn(h_up[2:], -1)]
            own_all = [hz, h_up] + h_far + [h_down]
            oth_all = [swap(h) for h in own_all]

    flip = jnp.stack([core, 1 - core]).astype(jnp.int32)
    parts = [h.reshape(-1, half) for h in own_all + oth_all]
    grad_weight = pl.pallas_call(
        _dw_kernel,
        out_shape=jax.ShapeDtypeStruct((9, 2 * half, 128), F32),
        grid_spec=pltpu.PrefetchScalarGridSpec(
            num_scalar_prefetch=1, grid=(4,),
            in_specs=[pl.BlockSpec((p.shape[0], 128), lambda i, c: (0, i)) for p in parts] + [pl.BlockSpec((4, PIX, 128), lambda i, c: (0, 0, 0))] * 4,
            out_specs=pl.BlockSpec((9, 256, 128), lambda i, c: (0, i, 0)),
            scratch_shapes=[pltpu.VMEM((3, PIX + 2 * SIDE, 128), BF), pltpu.VMEM((16 * PIX, 9 * 128), BF)]),
        compiler_params=_limit(52), name="dw",
    )(flip, *parts, *dall)

    small = jnp.transpose(jnp.concatenate([gain_sum, bias_sum], axis=0).reshape(2, 4, 128), (1, 0, 2))
    total = lax.dynamic_index_in_dim(small, z, 0, keepdims=False)
    for by in (1, 2, 3):
        piece = lax.dynamic_index_in_dim(small, (z + by) % 4, 0, keepdims=False)
        total = total + turn_z(piece, by)
    total, grad_weight = lax.optimization_barrier((total, grad_weight))
    small = total + turn(total, 1) + turn(total, 2) + turn(total, -1)
    return (grad_weight[None], small[0:1], small[1:2])


def solution(mesh):
    in_specs = (
        P(None, "dp", None, "chan"),
        P(None, "dp", None, "chan"),
        P("segment", None, None, "chan"),
        P("segment", "chan"),
        P("segment", "chan"),
    )
    out_specs = (P("segment", None, None, "chan"), P("segment", "chan"), P("segment", "chan"))

    return jax.shard_map(local, mesh=mesh, in_specs=in_specs, out_specs=out_specs, check_vma=False)
```

```python
import jax
import jax.numpy as jnp
from jax import lax
from jax.experimental import pallas as pl
from jax.experimental.pallas import tpu as pltpu
from jax.sharding import PartitionSpec as P


GROUPS = 32
SIDE = 16
EPSILON = 1e-05
PIX = SIDE * SIDE
BF = jnp.bfloat16
F32 = jnp.float32


def _groups(width):
    r = lax.broadcasted_iota(jnp.int32, (128, 128), 0) // width
    c = lax.broadcasted_iota(jnp.int32, (128, 128), 1) // width
    return jnp.where(r == c, 1.0, 0.0).astype(BF)


def _group_sum(v, ones):
    n = v.shape[1] // 128
    rows = jnp.concatenate([v[:, i * 128:(i + 1) * 128] for i in range(n)], axis=0)
    hi = rows.astype(BF)
    rest = rows - hi.astype(F32)
    mid = rest.astype(BF)
    low = (rest - mid.astype(F32)).astype(BF)
    out = (jnp.dot(hi, ones, preferred_element_type=F32)
           + jnp.dot(mid, ones, preferred_element_type=F32)
           + jnp.dot(low, ones, preferred_element_type=F32))
    return jnp.concatenate([out[i:i + 1] for i in range(n)], axis=1)


def _normalized(a, count, width):
    ones = _groups(width)
    v = a.astype(F32)
    mean = _group_sum(jnp.sum(v, axis=0, keepdims=True), ones) * (1.0 / count)
    cen = v - mean
    var = _group_sum(jnp.sum(cen * cen, axis=0, keepdims=True), ones) * (1.0 / count)
    rstd = lax.rsqrt(var + EPSILON)
    return cen * rstd, rstd


def _gn_kernel(width, a_ref, gain_ref, bias_ref, h_ref):
    xhat, _ = _normalized(a_ref[...], PIX * width, width)
    n = xhat * gain_ref[...] + bias_ref[...]
    h_ref[...] = (n * jax.nn.sigmoid(n)).astype(BF)


def _prep_kernel(width, a_ref, gain_ref, bias_ref, h_ref, xhat_ref, slope_ref, rstd_ref):
    xhat, rstd = _normalized(a_ref[...], PIX * width, width)
    n = xhat * gain_ref[...] + bias_ref[...]
    s = jax.nn.sigmoid(n)
    h_ref[...] = (n * s).astype(BF)
    xhat_ref[...] = xhat
    slope_ref[...] = s * (1.0 + n * (1.0 - s))
    rstd_ref[...] = rstd


def _gn_bwd_kernel(width, dy_ref, own_ref, oth_ref, xhat_ref, slope_ref, rstd_ref, gain_ref,
                   da_ref, dg_ref, db_ref):
    ones = _groups(width)
    count = PIX * width
    dn = (own_ref[...] + oth_ref[...].astype(F32)) * slope_ref[...]
    xhat = xhat_ref[...]
    gain = gain_ref[...]
    db = jnp.sum(dn, axis=0, keepdims=True)
    dg = jnp.sum(dn * xhat, axis=0, keepdims=True)
    m1 = _group_sum(db * gain, ones) * (1.0 / count)
    m2 = _group_sum(dg * gain, ones) * (1.0 / count)
    da = dy_ref[...].astype(F32) + rstd_ref[...] * (dn * gain - m1 - xhat * m2)
    da_ref[...] = da.astype(BF)
    dg_ref[...] = dg
    db_ref[...] = db


def _pad_into(ref, value):
    zero = jnp.zeros((SIDE, ref.shape[1]), ref.dtype)
    ref[0:SIDE, :] = zero
    ref[SIDE:SIDE + PIX, :] = value
    ref[SIDE + PIX:, :] = zero


def _join_shifts(left, mid, right):
    x = lax.broadcasted_iota(jnp.int32, mid.shape, 0) % SIDE
    out = mid + jnp.where(x > 0, pltpu.roll(left, 1, 0), 0.0)
    return out + jnp.where(x < SIDE - 1, pltpu.roll(right, PIX - 1, 0), 0.0)


def _cat_into(ref, col, value, turn):
    wide = value.shape[1]
    zero = jnp.zeros((SIDE, wide), value.dtype)
    for ky in range(3):
        lo = ky * (ref.shape[1] // 3) + col
        by = (ky - 1) * turn
        if by == 0:
            ref[:, lo:lo + wide] = value
        elif by < 0:
            ref[0:SIDE, lo:lo + wide] = zero
            ref[SIDE:, lo:lo + wide] = value[:PIX - SIDE]
        else:
            ref[0:PIX - SIDE, lo:lo + wide] = value[SIDE:]
            ref[PIX - SIDE:, lo:lo + wide] = zero


def _conv_kernel(on_ref, own_ref, oth_ref, a_ref, w_ref, y_ref, cat_ref, acc_ref):
    kx = pl.program_id(0)

    @pl.when(on_ref[0] > 0)
    def _():
        _conv_step(kx, own_ref, oth_ref, a_ref, w_ref, y_ref, cat_ref, acc_ref)

    @pl.when((on_ref[0] == 0) & (kx == 0))
    def _():
        y_ref[...] = jnp.zeros_like(y_ref)


def _conv_step(kx, own_ref, oth_ref, a_ref, w_ref, y_ref, cat_ref, acc_ref):

    @pl.when(kx == 0)
    def _():
        _cat_into(cat_ref, 0, own_ref[...], 1)
        _cat_into(cat_ref, own_ref.shape[1], oth_ref[...], 1)

    acc_ref[kx] = jnp.dot(cat_ref[...], w_ref[0], preferred_element_type=F32)

    @pl.when(kx == 2)
    def _():
        z = _join_shifts(acc_ref[0], acc_ref[1], acc_ref[2])
        y_ref[...] = (a_ref[...].astype(F32) + z).astype(BF)


def _dgrad_kernel(on_ref, dy_ref, w_ref, own_ref, oth_ref, cat_ref, acc_ref):
    kx = pl.program_id(0)

    @pl.when(on_ref[0] > 0)
    def _():
        _dgrad_step(kx, dy_ref, w_ref, own_ref, oth_ref, cat_ref, acc_ref)

    @pl.when((on_ref[0] == 0) & (kx == 0))
    def _():
        own_ref[...] = jnp.zeros_like(own_ref)
        oth_ref[...] = jnp.zeros_like(oth_ref)


def _dgrad_step(kx, dy_ref, w_ref, own_ref, oth_ref, cat_ref, acc_ref):

    @pl.when(kx == 0)
    def _():
        _cat_into(cat_ref, 0, dy_ref[...], -1)

    acc_ref[kx] = jnp.dot(cat_ref[...], w_ref[0], preferred_element_type=F32)

    @pl.when(kx == 2)
    def _():
        half = dy_ref.shape[1]
        p = _join_shifts(acc_ref[2], acc_ref[1], acc_ref[0])
        own_ref[...] = p[:, :half]
        oth_ref[...] = p[:, half:].astype(BF)


def _dw_kernel(idx_ref, *refs):
    own, oth, dys = refs[0:5], refs[5:10], refs[10:14]
    out_ref, pad_ref, rhs_ref = refs[14:]

    @pl.when(pl.program_id(0) == 0)
    def _():
        x = lax.broadcasted_iota(jnp.int32, (PIX, 128), 0) % SIDE
        for g in range(4):
            def build(i, carry):
                v = dys[g][i].astype(F32)
                moved = (jnp.where(x < SIDE - 1, pltpu.roll(v, PIX - 1, 0), 0.0), v,
                         jnp.where(x > 0, pltpu.roll(v, 1, 0), 0.0))
                for kx in range(3):
                    _pad_into(pad_ref.at[kx], moved[kx].astype(BF))
                for t in range(9):
                    start = (2 - t // 3) * SIDE
                    at = pl.multiple_of((g * 4 + i) * PIX, PIX)
                    rhs_ref[pl.ds(at, PIX), t * 128:(t + 1) * 128] = pad_ref[t % 3, start:start + PIX, :]
                return carry

            lax.fori_loop(0, 4, build, 0)

    h = jnp.concatenate([jnp.concatenate([p[...], q[...]], axis=1) for p, q in zip(own, oth)], axis=0)
    for lo, taps in ((0, 2), (2, 2), (4, 2), (6, 2), (8, 1)):
        part = lax.dot_general(h, rhs_ref[:, lo * 128:(lo + taps) * 128], (((0,), (0,)), ((), ())),
                               preferred_element_type=F32)
        for i in range(taps):
            for side in range(2):
                at = pl.multiple_of(idx_ref[side] * 128, 128)
                out_ref[lo + i, pl.ds(at, 128), :] = part[side * 128:(side + 1) * 128, i * 128:(i + 1) * 128]


def _assemble_kernel(idx_ref, near, up, down, far0, far1, *rest):
    out_ref = rest[-1]
    for side in range(2):
        at = idx_ref[4 + side]
        for kx in range(3):
            out_ref[kx, 0, at, idx_ref[0]] = near[side, kx]
            out_ref[kx, 0, at, idx_ref[1]] = up[side, kx]
            out_ref[kx, 0, at, idx_ref[2]] = (far0, far1)[side][kx]
            out_ref[kx, 0, at, idx_ref[3]] = down[side, kx]


def _place_kernel(idx_ref, *refs):
    for by in range(4):
        refs[4][:, pl.ds(pl.multiple_of(idx_ref[by] * 128, 128), 128)] = refs[by][...]


def _limit(mib):
    return pltpu.CompilerParams(vmem_limit_bytes=mib << 20)


def local(x_input, d_output, weights, gains, biases):
    row = lax.axis_index("dp")
    segment = lax.axis_index("segment")
    chan = lax.axis_index("chan")
    z = chan // 2
    core = chan % 2
    width = weights.shape[2] // GROUPS
    half = 4 * 128
    axes = ("dp", "segment", "chan")

    def lin(d, s, k):
        return (d * 8 + s) * 8 + k

    def move(value, source, target):
        flip = (source < 4) != (target < 4)
        pairs = [(lin(d, source, k), lin(d, target, (6 - k + 2 * (k % 2)) if flip else k))
                 for d in range(4) for k in range(8)]
        return lax.ppermute(value, axes, pairs)

    def swap(value):
        return lax.ppermute(value, "chan", [(k, k ^ 1) for k in range(8)])

    def turn(value, by):
        return lax.ppermute(value, "dp", [(i, (i + by) % 4) for i in range(4)])

    def turn_z(value, by):
        return lax.ppermute(value, "chan", [(k, (k + 2 * by) % 8) for k in range(8)])

    sources = ((z - jnp.arange(4)) % 4).astype(jnp.int32)

    def send(pick):
        return [pick(z)] + [turn_z(pick((z + by) % 4), by) for by in (1, 2, 3)]

    def place(parts):
        shape = jax.ShapeDtypeStruct((parts[0].shape[0], half), parts[0].dtype)
        return pl.pallas_call(
            _place_kernel, out_shape=shape,
            grid_spec=pltpu.PrefetchScalarGridSpec(
                num_scalar_prefetch=1, grid=(1,),
                in_specs=[pl.BlockSpec(parts[0].shape, lambda t, i: (0, 0))] * 4,
                out_specs=pl.BlockSpec(shape.shape, lambda t, i: (0, 0))),
            compiler_params=_limit(6), name="place")(sources, *parts)

    rows = jnp.concatenate([gains, biases], axis=0)
    rows = send(lambda t: rows)
    first = send(lambda t: lax.dynamic_index_in_dim(x_input[:, 0], t, 0, keepdims=False))

    quarter = lax.dynamic_slice_in_dim(weights[0], row * 256, 256, 1)
    quarter = jnp.transpose(quarter.reshape(9, 2, 128, 128), (1, 0, 2, 3))
    rows, first, quarter = lax.optimization_barrier((rows, first, quarter))
    rows = place(rows)
    first = place(first)
    sides = [(row + jnp.arange(4)) % 4, (core + jnp.arange(2)) % 2]
    token = None
    pieces = {}

    def assemble(by, w=None):
        places = jnp.concatenate(sides + [(z - by)[None] % 4]).astype(jnp.int32)
        return pl.pallas_call(
            _assemble_kernel,
            out_shape=jax.ShapeDtypeStruct((3, 3, 2, 4, 128, half), BF),
            grid_spec=pltpu.PrefetchScalarGridSpec(
                num_scalar_prefetch=1, grid=(3,),
                in_specs=[pl.BlockSpec((2, 3, 128, 128), lambda t, i: (0, t, 0, 0))] * 3
                + [pl.BlockSpec((3, 128, 128), lambda t, i: (t, 0, 0))] * 2
                + ([] if w is None else [pl.BlockSpec(memory_space=pl.ANY)]),
                out_specs=pl.BlockSpec((3, 1, 2, 4, 128, 128), lambda t, i: (0, t, 0, 0, 0, i[6]))),
            input_output_aliases={} if w is None else {6: 0},
            compiler_params=_limit(52), name="assemble",
        )(places, *pieces[by], *([] if w is None else [w]))

    for by in (0, 1, 3, 2):
        piece = quarter
        if by > 1:
            piece, token = lax.optimization_barrier((piece, token))
        if by > 0:
            piece = turn_z(piece, by)
        if by == 1:
            piece, rows, first = lax.optimization_barrier((piece, rows, first))
        token = piece
        below = turn(piece, 1)
        above = turn(piece, -1)
        far = [turn(below[0], 1), turn(above[1], -1)]
        pieces[by] = [piece, above, below] + far
    w = None
    for by in (0, 1, 3, 2):
        w = assemble(by, w)
    w = w.reshape(3, 6 * half, half)

    gain = rows[0:1]
    bias = rows[1:2]

    act = jax.ShapeDtypeStruct((PIX, half), BF)
    act32 = jax.ShapeDtypeStruct((PIX, half), F32)
    line = jax.ShapeDtypeStruct((1, half), F32)

    def normed(a):
        return pl.pallas_call(lambda *r: _gn_kernel(width, *r), out_shape=act, compiler_params=_limit(6), name="gn")(a, gain, bias)

    def prep(a):
        return pl.pallas_call(lambda *r: _prep_kernel(width, *r), out_shape=(act, act32, act32, line),
                              compiler_params=_limit(10), name="prep")(a, gain, bias)

    full = pl.BlockSpec((PIX, half), lambda t, on: (0, 0))

    def turn_on(j):
        return jnp.where(segment == j, 1, 0).astype(jnp.int32).reshape(1)

    def conv(j, own, oth, a):
        return pl.pallas_call(
            _conv_kernel, out_shape=act,
            grid_spec=pltpu.PrefetchScalarGridSpec(
                num_scalar_prefetch=1, grid=(3,),
                in_specs=[full, full, full, pl.BlockSpec((1, 6 * half, half), lambda t, on: (t * on[0], 0, 0))],
                out_specs=full,
                scratch_shapes=[pltpu.VMEM((PIX, 6 * half), BF), pltpu.VMEM((3, PIX, half), F32)]),
            compiler_params=_limit(52), name="conv")(turn_on(j), own, oth, a, w)

    def dgrad(j, dy):
        return pl.pallas_call(
            _dgrad_kernel, out_shape=(act32, act),
            grid_spec=pltpu.PrefetchScalarGridSpec(
                num_scalar_prefetch=1, grid=(3,),
                in_specs=[full, pl.BlockSpec((1, 3 * half, 2 * half), lambda t, on: (t * on[0], 0, 0))],
                out_specs=(full, full),
                scratch_shapes=[pltpu.VMEM((PIX, 3 * half), BF), pltpu.VMEM((3, PIX, 2 * half), F32)]),
            compiler_params=_limit(52), name="dgrad")(turn_on(j), dy, w_turned)

    def added(p, q):
        return (p.astype(F32) + q.astype(F32)).astype(BF)

    first, gain, bias, w = lax.optimization_barrier((first, gain, bias, w))
    a = jnp.where(segment == 0, first, jnp.zeros_like(first))
    inputs = [a]
    skips = {}
    for j in range(7):
        own = normed(a)
        oth = swap(own)
        y = conv(j, own, oth, a)
        if j == 1:
            late, end, y = lax.optimization_barrier((w, d_output[:, 0], y))
            last = place(send(lambda t: lax.dynamic_index_in_dim(end, 3 - t, 0, keepdims=False)))
            late = jnp.transpose(late.reshape(3, 3, 2 * half, half), (0, 1, 3, 2))
        a = move(y, j, j + 1)
        if j == 1:
            late, last, a = lax.optimization_barrier((late, last, a))
        if j < 3:
            skips[j] = move(y, j, 7 - j)
        if j >= 4:
            a = added(a, skips[6 - j])
        inputs.append(a)
    mine = inputs[0]
    for a in inputs[1:]:
        mine = mine + a

    hidden, xhat, slope, rstd = prep(mine)
    w_turned = late.reshape(3, 3 * half, 2 * half)

    dy = jnp.where(segment == 7, last, jnp.zeros_like(last))
    grads = []
    gain_sum = bias_sum = 0.0
    skip_grads = {}
    for j in reversed(range(8)):
        if j == 0:
            mine = grads[0]
            for g in grads[1:]:
                mine = mine + g
            mine = mine + dy
            dz = [lax.dynamic_slice_in_dim(mine, (z + by) % 4 * 128, 128, 1) for by in range(4)]
            dz = jnp.stack(dz[:1] + [turn_z(dz[by], by) for by in (1, 2, 3)])
            dz, dy = lax.optimization_barrier((dz, dy))
            turned = [turn(dz, -1), turn(dz, 2), turn(dz, 1)]
            dall = [dz] + turned
        grads.append(dy)
        own, oth = dgrad(j, dy)
        oth = swap(oth)
        da, dg, db = pl.pallas_call(
            lambda *r: _gn_bwd_kernel(width, *r), out_shape=(act, line, line),
            compiler_params=_limit(10), name="gn_bwd",
        )(dy, own, oth, xhat, slope, rstd, gain)
        gain_sum = gain_sum + dg
        bias_sum = bias_sum + db
        if j > 0:
            dy = move(da, j, j - 1)
        if j > 4:
            skip_grads[7 - j] = move(da, j, 7 - j)
        if 0 < j < 4:
            dy = added(dy, skip_grads[j - 1])
        if j == 4:
            hidden, dg = lax.optimization_barrier((hidden, dg))
            hz = jnp.stack([hidden] + [turn_z(hidden, by) for by in (1, 2, 3)])
            _, dy = lax.optimization_barrier((hz, dy))
            h_up = turn(hz, -1)
            h_down = turn(hz, 1)
            h_far = [turn(h_down[:2], 1), turn(h_up[2:], -1)]
            own_all = [hz, h_up] + h_far + [h_down]
            near = [swap(h) for h in (hz, h_up, h_down)]
            oth_all = near[:2] + [swap(h) for h in h_far] + near[2:]

    flip = jnp.stack([core, 1 - core]).astype(jnp.int32)
    parts = [h.reshape(-1, half) for h in own_all + oth_all]
    grad_weight = pl.pallas_call(
        _dw_kernel,
        out_shape=jax.ShapeDtypeStruct((9, 2 * half, 128), F32),
        grid_spec=pltpu.PrefetchScalarGridSpec(
            num_scalar_prefetch=1, grid=(4,),
            in_specs=[pl.BlockSpec((p.shape[0], 128), lambda i, c: (0, i)) for p in parts] + [pl.BlockSpec((4, PIX, 128), lambda i, c: (0, 0, 0))] * 4,
            out_specs=pl.BlockSpec((9, 256, 128), lambda i, c: (0, i, 0)),
            scratch_shapes=[pltpu.VMEM((3, PIX + 2 * SIDE, 128), BF), pltpu.VMEM((16 * PIX, 9 * 128), BF)]),
        compiler_params=_limit(52), name="dw",
    )(flip, *parts, *dall)

    small = jnp.transpose(jnp.concatenate([gain_sum, bias_sum], axis=0).reshape(2, 4, 128), (1, 0, 2))
    sums = [lax.dynamic_index_in_dim(small, (z + by) % 4, 0, keepdims=False) for by in range(4)]
    sums = sums[:1] + [turn_z(sums[by], by) for by in (1, 2, 3)]
    sums, grad_weight = lax.optimization_barrier((sums, grad_weight))
    total = sums[0] + sums[1] + sums[2] + sums[3]
    small = total + turn(total, 1) + turn(total, 2) + turn(total, -1)
    return (grad_weight[None], small[0:1], small[1:2])


def solution(mesh):
    in_specs = (
        P(None, "dp", None, "chan"),
        P(None, "dp", None, "chan"),
        P("segment", None, None, "chan"),
        P("segment", "chan"),
        P("segment", "chan"),
    )
    out_specs = (P("segment", None, None, "chan"), P("segment", "chan"), P("segment", "chan"))

    return jax.shard_map(local, mesh=mesh, in_specs=in_specs, out_specs=out_specs, check_vma=False)
```
